512 devices in a mesh: req: 128 (over x, z, core), tp: 4 (over y).
Axes of the slice: x: 4, y: 4, z: 16, core: 2. Of those that a mesh axis runs over, the one named last changes fastest.
Arguments:
- layer_input: bfloat16 [16384, 2048], P('req', 'tp'), may hold values from -6 to 6
- q_in: bfloat16 [16384, 1024], P('req', 'tp'), may hold values from -6 to 6
- k_in: bfloat16 [16384, 1024], P('req', 'tp'), may hold values from -6 to 6
- v_in: bfloat16 [16384, 2048], P('req', 'tp'), may hold values from -6 to 6
- z_in: bfloat16 [16384, 2048], P('req', 'tp'), may hold values from -6 to 6
- conv_q: bfloat16 [4, 1024], P(None, 'tp'), may hold values from -3 to 3
- conv_k: bfloat16 [4, 1024], P(None, 'tp'), may hold values from -3 to 3
- conv_v: bfloat16 [4, 2048], P(None, 'tp'), may hold values from -3 to 3
- gate_weight: bfloat16 [2048, 16], P('tp'), may hold values from -0.125 to 0.125
- decay_rate: float32 [8], P('tp'), may hold values from 0.0001 to 0.05
- dt_bias: float32 [8], P('tp'), may hold values from -1 to 1
- norm_gain: bfloat16 [256], replicated, may hold values from 0.099609375 to 1.8984375
- segment_ids: int32 [16384], P('req'), may hold values from 0 to 63, never falling along the last dimension, each value on 1 to 1024 neighbouring positions
Outputs:
- mixed: bfloat16 [16384, 2048], P('req', 'tp')
The draws below stay inside these ranges and needn't reach their ends.
Inputs may be any that keep to these rules, and one draw needn't show every extreme that they name: segment_ids never falls along the tokens; every prompt 0 to 63 has 1 to 1024 tokens, and one has exactly 1024.
All inputs are finite; a program needn't handle non-finite values.
Results may differ from the reference program's by a relative error of at most 0.0055.
Values may be sent and summed in bfloat16 or wider, within the bound.
A program may use at most 128 MiB of HBM per device.

```python
import math
import jax
import jax.numpy as jnp
import numpy as np
from jax import lax

D = 2048
HEADS = 8
DK = 128
DV = 256
CONV = 4
BLOCK = 64
TOKENS = 16384
MAX_LEN = 1024
REQUESTS = 64


def steps_of(stream_key, shape, cuts, smallest, largest):
    level = 1.0
    for position, shards_of in cuts:
        draws = jax.random.uniform(jax.random.fold_in(jax.random.fold_in(stream_key, 6), position), (shards_of,), jnp.float32, smallest / len(cuts), largest / len(cuts))
        level = level * jnp.repeat(jnp.exp(draws), shape[position] // shards_of).reshape((-1,) + (1,) * (len(shape) - 1 - position))
    return level


def length_profile(number_of, total, most, lean):
    weights = [(1 << 20) // math.isqrt(standing ** lean) + 1 for standing in range(2, number_of + 1)]
    surplus, holding = total - most - (number_of - 1), [1] * (number_of - 1)
    while surplus > 0:
        candidates = [i for i in range(number_of - 1) if holding[i] < most]
        pool, budget = sum([weights[i] for i in candidates]), surplus
        for i in candidates:
            extra = min(most - holding[i], max(1, budget * weights[i] // pool), surplus)
            holding[i] = holding[i] + extra
            surplus = surplus - extra
    return np.array([most] + holding)


def uneven(rng, number_of, total, most, skew):
    if number_of == 2:
        one = jax.random.randint(rng, (), max(1, total - most), min(most, total - 1) + 1)
        return jnp.stack([one, total - one])
    lengths = jnp.asarray(length_profile(number_of, total, most, skew), jnp.int32)
    pairs = (number_of - 1) // 2
    donor, sink = lengths[1:1 + 2 * pairs:2], lengths[2:2 + 2 * pairs:2]
    room = jnp.minimum(donor - 1, most - sink)
    moved = jax.random.randint(jax.random.fold_in(rng, 1), (pairs,), 0, 1 << 20) % (room + 1)
    lengths = lengths.at[1:1 + 2 * pairs:2].set(donor - moved).at[2:2 + 2 * pairs:2].set(sink + moved)
    return lengths[jax.random.permutation(jax.random.fold_in(rng, 2), number_of)]


def centred(stream_key, extent, scale, most, shards=(), kind=jnp.bfloat16):
    factor_of = steps_of(stream_key, extent, shards, -0.22, 0.18) if shards else 1.0
    drawn = jax.random.normal(stream_key, extent, jnp.float32) * scale * factor_of
    return jnp.minimum(jnp.maximum(drawn, -most), most).astype(kind)


def setup_inputs(seed: int = 0) -> dict:
    arg_keys = jax.random.split(jax.random.key(seed), 14)
    return {
        "layer_input": centred(arg_keys[0], (TOKENS, D), 1.0, 6.0, ((0, 128), (1, 4))),
        "q_in": centred(arg_keys[1], (TOKENS, HEADS * DK), 1.0, 6.0, ((0, 128), (1, 4))),
        "k_in": centred(arg_keys[2], (TOKENS, HEADS * DK), 1.0, 6.0, ((0, 128), (1, 4))),
        "v_in": centred(arg_keys[3], (TOKENS, HEADS * DV), 1.0, 6.0, ((0, 128), (1, 4))),
        "z_in": centred(arg_keys[4], (TOKENS, HEADS * DV), 1.0, 6.0, ((0, 128), (1, 4))),
        "conv_q": centred(arg_keys[5], (CONV, HEADS * DK), CONV ** -0.5, 3.0, ((1, 4),)),
        "conv_k": centred(arg_keys[6], (CONV, HEADS * DK), CONV ** -0.5, 3.0, ((1, 4),)),
        "conv_v": centred(arg_keys[7], (CONV, HEADS * DV), CONV ** -0.5, 3.0, ((1, 4),)),
        "gate_weight": centred(arg_keys[8], (D, 2 * HEADS), D ** -0.5, 0.125, ((0, 4),)),
        "decay_rate": jnp.clip(jnp.exp(math.log(0.05) - 6.214608 * jax.random.uniform(arg_keys[9], (HEADS,), jnp.float32) ** steps_of(arg_keys[9], (HEADS,), ((0, 4),), -0.2, 0.2)), 0.0001, 0.05),
        "dt_bias": jnp.clip(jax.random.uniform(arg_keys[10], (HEADS,), jnp.float32, -1.0, 1.0) * steps_of(arg_keys[10], (HEADS,), ((0, 4),), -0.4, 0.0), -1.0, 1.0),
        "norm_gain": jnp.clip(1.0 + 0.18 * jax.random.normal(arg_keys[11], (DV,), jnp.float32), 0.099609375, 1.8984375).astype(jnp.bfloat16),
        "segment_ids": jnp.searchsorted(jnp.cumsum(uneven(arg_keys[12], REQUESTS, TOKENS, MAX_LEN, 2)), jnp.arange(TOKENS), side="right").astype(jnp.int32),
    }


highest = lax.Precision.HIGHEST

def product(pattern, first_op, second_op):
    return jnp.einsum(pattern, first_op, second_op, precision=highest)

def short_conv(extended, seg_ext, weight, row_count):
    own_seg = seg_ext[CONV - 1:]
    summed = jnp.zeros((row_count, extended.shape[1]), jnp.float32)
    for offset in range(CONV):
        same_req = (seg_ext[offset:offset + row_count] == own_seg)[:, None]
        summed = summed + jnp.where(same_req, extended[offset:offset + row_count], 0.0) * weight[offset].astype(jnp.float32)
    return jax.nn.silu(summed)

def unit_keys(key_raw, heads):
    shaped = key_raw.reshape(key_raw.shape[0], heads, DK)
    return shaped * lax.rsqrt(lax.optimization_barrier(jnp.sum(shaped * shaped, axis=2, keepdims=True)) + 1e-06)

def block_terms(queries, keyset, values, log_alpha, beta_gate, seg_block, seg_before):
    length = seg_block.shape[0]
    width = values.shape[2]
    cumulative = jnp.cumsum(log_alpha, axis=0)
    positions = jnp.arange(length)
    same_req = seg_block[:, None] == seg_block[None, :]
    causal = (positions[:, None] >= positions[None, :]) & same_req
    strict = (positions[:, None] > positions[None, :]) & same_req
    gap_log = jnp.transpose(cumulative[:, None, :] - cumulative[None, :, :], (2, 0, 1))
    decays = jnp.where(causal[None], jnp.exp(jnp.where(causal[None], gap_log, 0.0)), 0.0)
    linked = (seg_block == seg_before).astype(jnp.float32)
    tail_mask = (seg_block == seg_block[length - 1]).astype(jnp.float32)
    key_dots = product('ihd,jhd->hij', keyset, keyset)
    coupling = jnp.transpose(beta_gate)[:, :, None] * key_dots * jnp.where(strict[None], decays, 0.0)
    system = jnp.eye(length, dtype=jnp.float32)[None] + coupling
    start_scale = jnp.exp(cumulative) * linked[:, None]
    right_side = jnp.concatenate([beta_gate[:, :, None] * values, (beta_gate * start_scale)[:, :, None] * keyset], axis=2)
    solved = lax.linalg.triangular_solve(system, jnp.transpose(right_side, (1, 0, 2)), left_side=True, lower=True)
    fresh_part = solved[:, :, :width]
    carried = solved[:, :, width:]
    scores = product('ihd,jhd->hij', queries, keyset) * decays
    reach_back = jnp.transpose(queries * start_scale[:, :, None], (1, 0, 2)) - product('hij,hjd->hid', scores, carried)
    local_out = product('hij,hjd->hid', scores, fresh_part)
    fade_out = jnp.exp(cumulative[length - 1][None, :] - cumulative) * tail_mask[:, None]
    pushed = jnp.transpose(fade_out[:, :, None] * keyset, (1, 0, 2))
    keep_scale = linked[length - 1] * jnp.exp(cumulative[length - 1])
    carry_map = keep_scale[:, None, None] * jnp.eye(keyset.shape[2], dtype=jnp.float32)[None] - product('hcd,hce->hde', pushed, carried)
    injected = product('hcd,hce->hde', pushed, fresh_part)
    return (local_out, reach_back, carry_map, injected)

def finish(outputs, z_part, norm_gain):
    scale = lax.rsqrt(lax.optimization_barrier(jnp.mean(outputs * outputs, axis=2, keepdims=True)) + 1e-06)
    gating = jax.nn.silu(z_part.astype(jnp.float32).reshape(outputs.shape))
    result = outputs * scale * norm_gain.astype(jnp.float32)[None, None, :] * gating
    return result.astype(jnp.bfloat16).reshape(outputs.shape[0], -1)

def reference(layer_input, q_in, k_in, v_in, z_in, conv_q, conv_k, conv_v, gate_weight, decay_rate, dt_bias, norm_gain, segment_ids):
    gate_total = jnp.dot(layer_input.astype(jnp.float32), gate_weight.astype(jnp.float32), preferred_element_type=jnp.float32)
    log_alpha = -decay_rate[None, :] * jax.nn.softplus(gate_total[:, :HEADS] + dt_bias[None, :])
    beta_gate = jax.nn.sigmoid(gate_total[:, HEADS:])
    block_count = TOKENS // BLOCK
    edge_rows = CONV - 1

    def blocks(array):
        return array.reshape((block_count, BLOCK) + array.shape[1:])

    def advance(running, block_data):
        state_now, tail_q, tail_k, tail_v, tail_seg = running
        q_part, k_part, v_part, z_part, alpha_part, beta_part, seg_part = block_data
        seg_ext = jnp.concatenate([tail_seg, seg_part])
        q_ext = jnp.concatenate([tail_q, q_part.astype(jnp.float32)])
        k_ext = jnp.concatenate([tail_k, k_part.astype(jnp.float32)])
        v_ext = jnp.concatenate([tail_v, v_part.astype(jnp.float32)])
        queries = short_conv(q_ext, seg_ext, conv_q, BLOCK).reshape(BLOCK, HEADS, DK)
        keyset = unit_keys(short_conv(k_ext, seg_ext, conv_k, BLOCK), HEADS)
        values = short_conv(v_ext, seg_ext, conv_v, BLOCK).reshape(BLOCK, HEADS, DV)
        local_out, reach_back, carry_map, injected = block_terms(queries, keyset, values, alpha_part, beta_part, seg_part, tail_seg[edge_rows - 1])
        out_now = local_out + product('hcd,hde->hce', reach_back, state_now)
        next_state = product('hde,hef->hdf', carry_map, state_now) + injected
        mixed_part = finish(jnp.transpose(out_now, (1, 0, 2)), z_part, norm_gain)
        return ((next_state, q_ext[BLOCK:], k_ext[BLOCK:], v_ext[BLOCK:], seg_ext[BLOCK:]), mixed_part)
    start = (jnp.zeros((HEADS, DK, DV), jnp.float32), jnp.zeros((edge_rows, HEADS * DK), jnp.float32), jnp.zeros((edge_rows, HEADS * DK), jnp.float32), jnp.zeros((edge_rows, HEADS * DV), jnp.float32), jnp.full((edge_rows,), -1, jnp.int32))
    block_data = (blocks(q_in), blocks(k_in), blocks(v_in), blocks(z_in), blocks(log_alpha), blocks(beta_gate), blocks(segment_ids))
    final_state, mixed = lax.scan(advance, start, block_data)
    return mixed.reshape(TOKENS, HEADS * DV)
```

```python
import functools

import jax
import jax.numpy as jnp
from jax import lax
from jax.experimental import pallas as pl
from jax.experimental.pallas import tpu as pltpu
from jax.sharding import PartitionSpec as P

HEADS = 8
DK = 128
DV = 256
CONV = 4
BLOCK = 64


highest = lax.Precision.HIGHEST


def passed_along(value, axis, by):
    devices = lax.axis_size(axis)
    pairs = [(i, i + by) for i in range(devices) if 0 <= i + by < devices]
    return lax.ppermute(value, axis, pairs)


def product(pattern, first_op, second_op):
    return jnp.einsum(pattern, first_op, second_op, precision=highest)


def short_conv(extended, seg_ext, weight, row_count):
    own_seg = seg_ext[CONV - 1 :]
    summed = jnp.zeros((row_count, extended.shape[1]), jnp.float32)
    for offset in range(CONV):
        same_req = (seg_ext[offset : offset + row_count] == own_seg)[:, None]
        summed = summed + jnp.where(same_req, extended[offset : offset + row_count], 0.0) * weight[
            offset
        ].astype(jnp.float32)
    return jax.nn.silu(summed)


def unit_keys(key_raw, heads):
    shaped = key_raw.reshape(key_raw.shape[0], heads, DK)
    return shaped * lax.rsqrt(jnp.sum(shaped * shaped, axis=2, keepdims=True) + 1e-06)


def block_terms(queries, keyset, values, log_alpha, beta_gate, seg_block, seg_before):
    length = seg_block.shape[0]
    width = values.shape[2]
    cumulative = jnp.cumsum(log_alpha, axis=0)
    positions = jnp.arange(length)
    same_req = seg_block[:, None] == seg_block[None, :]
    causal = (positions[:, None] >= positions[None, :]) & same_req
    strict = (positions[:, None] > positions[None, :]) & same_req
    gap_log = jnp.transpose(cumulative[:, None, :] - cumulative[None, :, :], (2, 0, 1))
    decays = jnp.where(causal[None], jnp.exp(jnp.where(causal[None], gap_log, 0.0)), 0.0)
    linked = (seg_block == seg_before).astype(jnp.float32)
    tail_mask = (seg_block == seg_block[length - 1]).astype(jnp.float32)
    key_dots = product("ihd,jhd->hij", keyset, keyset)
    coupling = (
        jnp.transpose(beta_gate)[:, :, None] * key_dots * jnp.where(strict[None], decays, 0.0)
    )
    system = jnp.eye(length, dtype=jnp.float32)[None] + coupling
    start_scale = jnp.exp(cumulative) * linked[:, None]
    right_side = jnp.concatenate(
        [beta_gate[:, :, None] * values, (beta_gate * start_scale)[:, :, None] * keyset], axis=2
    )
    solved = lax.linalg.triangular_solve(
        system, jnp.transpose(right_side, (1, 0, 2)), left_side=True, lower=True
    )
    fresh_part = solved[:, :, :width]
    carried = solved[:, :, width:]
    scores = product("ihd,jhd->hij", queries, keyset) * decays
    reach_back = jnp.transpose(queries * start_scale[:, :, None], (1, 0, 2)) - product(
        "hij,hjd->hid", scores, carried
    )
    local_out = product("hij,hjd->hid", scores, fresh_part)
    fade_out = jnp.exp(cumulative[length - 1][None, :] - cumulative) * tail_mask[:, None]
    pushed = jnp.transpose(fade_out[:, :, None] * keyset, (1, 0, 2))
    keep_scale = linked[length - 1] * jnp.exp(cumulative[length - 1])
    carry_map = keep_scale[:, None, None] * jnp.eye(keyset.shape[2], dtype=jnp.float32)[
        None
    ] - product("hcd,hce->hde", pushed, carried)
    injected = product("hcd,hce->hde", pushed, fresh_part)
    return (local_out, reach_back, carry_map, injected)


def finish(outputs, z_part, norm_gain):
    scale = lax.rsqrt(jnp.mean(outputs * outputs, axis=2, keepdims=True) + 1e-06)
    gating = jax.nn.silu(z_part.astype(jnp.float32).reshape(outputs.shape))
    result = outputs * scale * norm_gain.astype(jnp.float32)[None, None, :] * gating
    return result.astype(jnp.bfloat16).reshape(outputs.shape[0], -1)


MESH = pl.DeviceIdType.MESH
SHIFTS = (1, 2, 4, 1)


def fold(high, low):
    return jnp.dot(high, low, precision=highest, preferred_element_type=jnp.float32)


def chain_kernel(
    devices, carry_ref, inject_ref, out_ref,
    got_a1, got_b1, got_a2, got_b2, got_b3,
    own_a2, own_b2, own_a4, own_b4, own_b8,
    send_sems, recv_sems,
):
    me = lax.axis_index("req")
    tp_me = lax.axis_index("tp")
    heads = carry_ref.shape[0]

    barrier = pltpu.get_barrier_semaphore()
    for shift in (1, 2, 4):
        for peer in (me + shift, me - shift):
            pl.semaphore_signal(
                barrier, inc=1, device_id=(lax.rem(peer + devices, devices), tp_me),
                device_id_type=MESH,
            )
    pl.semaphore_wait(barrier, 6)

    def exchange(round_index, sources, targets):
        shift = SHIFTS[round_index]
        copies = []
        for slot, (src, dst) in enumerate(zip(sources, targets)):
            copies.append(
                pltpu.make_async_remote_copy(
                    src_ref=src,
                    dst_ref=dst,
                    send_sem=send_sems.at[round_index, slot],
                    recv_sem=recv_sems.at[round_index, slot],
                    device_id=(lax.rem(me + shift, devices), tp_me),
                    device_id_type=MESH,
                )
            )

        @pl.when(me + shift < devices)
        def _():
            for copy in copies:
                copy.start()

        @pl.when(me >= shift)
        def _():
            for copy in copies:
                copy.wait_recv()

        @pl.when(me < shift)
        def _():
            for dst in targets:
                dst[...] = jnp.zeros(dst.shape, dst.dtype)

        return copies

    def finish_sends(round_index, copies):
        shift = SHIFTS[round_index]

        @pl.when(me + shift < devices)
        def _():
            for copy in copies:
                copy.wait_send()

    sent = exchange(0, (carry_ref, inject_ref), (got_a1, got_b1))
    for h in range(heads):
        own_a2[h] = fold(carry_ref[h], got_a1[h])
        own_b2[h] = fold(carry_ref[h], got_b1[h]) + inject_ref[h]
    finish_sends(0, sent)
    sent = exchange(1, (own_a2, own_b2), (got_a2, got_b2))
    for h in range(heads):
        own_a4[h] = fold(own_a2[h], got_a2[h])
        own_b4[h] = fold(own_a2[h], got_b2[h]) + own_b2[h]
    finish_sends(1, sent)
    sent = exchange(2, (own_b4,), (got_b3,))
    for h in range(heads):
        own_b8[h] = fold(own_a4[h], got_b3[h]) + own_b4[h]
    finish_sends(2, sent)
    sent = exchange(3, (own_b8,), (out_ref,))
    finish_sends(3, sent)


def carried_in(carry_total, inject_total, devices):
    heads, dk, dv = inject_total.shape
    a_shape = pltpu.VMEM((heads, dk, dk), jnp.float32)
    b_shape = pltpu.VMEM((heads, dk, dv), jnp.float32)
    return pl.pallas_call(
        functools.partial(chain_kernel, devices),
        out_shape=jax.ShapeDtypeStruct((heads, dk, dv), jnp.float32),
        in_specs=[pl.BlockSpec(memory_space=pltpu.VMEM)] * 2,
        out_specs=pl.BlockSpec(memory_space=pltpu.VMEM),
        scratch_shapes=[
            a_shape, b_shape, a_shape, b_shape, b_shape,
            a_shape, b_shape, a_shape, b_shape, b_shape,
            pltpu.SemaphoreType.DMA((4, 2)),
            pltpu.SemaphoreType.DMA((4, 2)),
        ],
        compiler_params=pltpu.CompilerParams(collective_id=0, has_side_effects=True),
    )(carry_total, inject_total)


def local(
    layer_input,
    q_in,
    k_in,
    v_in,
    z_in,
    conv_q,
    conv_k,
    conv_v,
    gate_weight,
    decay_rate,
    dt_bias,
    norm_gain,
    segment_ids,
):
    row_count = q_in.shape[0]
    local_heads = q_in.shape[1] // DK
    edge_rows = CONV - 1
    seg_marks = (segment_ids[row_count - edge_rows :] + 1).astype(jnp.bfloat16)[:, None]
    q_width, k_width = q_in.shape[1], k_in.shape[1]
    edges = jnp.concatenate(
        [
            q_in[row_count - edge_rows :],
            k_in[row_count - edge_rows :],
            v_in[row_count - edge_rows :],
            seg_marks,
        ],
        axis=1,
    )
    prior = passed_along(edges, "req", 1)
    prior_q = prior[:, :q_width]
    prior_k = prior[:, q_width : q_width + k_width]
    prior_v = prior[:, q_width + k_width : -1]
    prior_seg = prior[:, -1].astype(jnp.int32) - 1
    seg_ext = jnp.concatenate([prior_seg, segment_ids])
    queries = short_conv(
        jnp.concatenate([prior_q, q_in]).astype(jnp.float32), seg_ext, conv_q, row_count
    )
    keyset = unit_keys(
        short_conv(
            jnp.concatenate([prior_k, k_in]).astype(jnp.float32), seg_ext, conv_k, row_count
        ),
        local_heads,
    )
    values = short_conv(
        jnp.concatenate([prior_v, v_in]).astype(jnp.float32), seg_ext, conv_v, row_count
    )
    partial_value = jnp.dot(layer_input, gate_weight, preferred_element_type=jnp.float32)
    gate_total = lax.psum(partial_value, "tp")
    head_start = lax.axis_index("tp") * local_heads
    decay_in = lax.dynamic_slice_in_dim(gate_total, head_start, local_heads, 1)
    beta_in = lax.dynamic_slice_in_dim(gate_total, HEADS + head_start, local_heads, 1)
    log_alpha = -decay_rate[None, :] * jax.nn.softplus(decay_in + dt_bias[None, :])
    beta_gate = jax.nn.sigmoid(beta_in)
    local_out, reach_back, carry_map, injected = block_terms(
        queries.reshape(row_count, local_heads, DK),
        keyset,
        values.reshape(row_count, local_heads, DV),
        log_alpha,
        beta_gate,
        segment_ids,
        prior_seg[edge_rows - 1],
    )
    incoming = carried_in(carry_map, injected, lax.axis_size("req"))
    head_out = local_out + product("hcd,hde->hce", reach_back, incoming)
    head_out = jnp.transpose(head_out, (1, 0, 2))
    return finish(head_out, z_in, norm_gain)


def solution(mesh):
    placed = (
        P("req", "tp"),
        P("req", "tp"),
        P("req", "tp"),
        P("req", "tp"),
        P("req", "tp"),
        P(None, "tp"),
        P(None, "tp"),
        P(None, "tp"),
        P("tp", None),
        P("tp"),
        P("tp"),
        P(),
        P("req"),
    )
    return jax.shard_map(
        local, mesh=mesh, in_specs=placed, out_specs=P("req", "tp"), check_vma=False
    )
```

```python
import functools

import jax
import jax.numpy as jnp
from jax import lax
from jax.experimental import pallas as pl
from jax.experimental.pallas import tpu as pltpu
from jax.sharding import PartitionSpec as P

HEADS = 8
DK = 128
DV = 256
CONV = 4
BLOCK = 64


highest = lax.Precision.HIGHEST


def passed_along(value, axis, by):
    devices = lax.axis_size(axis)
    pairs = [(i, i + by) for i in range(devices) if 0 <= i + by < devices]
    return lax.ppermute(value, axis, pairs)


def product(pattern, first_op, second_op):
    return jnp.einsum(pattern, first_op, second_op, precision=highest)


def short_conv(extended, seg_ext, weight, row_count):
    own_seg = seg_ext[CONV - 1 :]
    summed = jnp.zeros((row_count, extended.shape[1]), jnp.float32)
    for offset in range(CONV):
        same_req = (seg_ext[offset : offset + row_count] == own_seg)[:, None]
        summed = summed + jnp.where(same_req, extended[offset : offset + row_count], 0.0) * weight[
            offset
        ].astype(jnp.float32)
    return jax.nn.silu(summed)


def unit_keys(key_raw, heads):
    shaped = key_raw.reshape(key_raw.shape[0], heads, DK)
    return shaped * lax.rsqrt(jnp.sum(shaped * shaped, axis=2, keepdims=True) + 1e-06)


def block_terms(queries, keyset, values, log_alpha, beta_gate, seg_block, seg_before):
    length = seg_block.shape[0]
    width = values.shape[2]
    cumulative = jnp.cumsum(log_alpha, axis=0)
    positions = jnp.arange(length)
    same_req = seg_block[:, None] == seg_block[None, :]
    causal = (positions[:, None] >= positions[None, :]) & same_req
    strict = (positions[:, None] > positions[None, :]) & same_req
    gap_log = jnp.transpose(cumulative[:, None, :] - cumulative[None, :, :], (2, 0, 1))
    decays = jnp.where(causal[None], jnp.exp(jnp.where(causal[None], gap_log, 0.0)), 0.0)
    linked = (seg_block == seg_before).astype(jnp.float32)
    tail_mask = (seg_block == seg_block[length - 1]).astype(jnp.float32)
    key_dots = product("ihd,jhd->hij", keyset, keyset)
    coupling = (
        jnp.transpose(beta_gate)[:, :, None] * key_dots * jnp.where(strict[None], decays, 0.0)
    )
    start_scale = jnp.exp(cumulative) * linked[:, None]
    right_side = jnp.concatenate(
        [beta_gate[:, :, None] * values, (beta_gate * start_scale)[:, :, None] * keyset], axis=2
    )
    solved = unit_lower_solve(coupling, jnp.transpose(right_side, (1, 0, 2)))
    fresh_part = solved[:, :, :width]
    carried = solved[:, :, width:]
    scores = product("ihd,jhd->hij", queries, keyset) * decays
    reach_back = jnp.transpose(queries * start_scale[:, :, None], (1, 0, 2)) - product(
        "hij,hjd->hid", scores, carried
    )
    local_out = product("hij,hjd->hid", scores, fresh_part)
    fade_out = jnp.exp(cumulative[length - 1][None, :] - cumulative) * tail_mask[:, None]
    pushed = jnp.transpose(fade_out[:, :, None] * keyset, (1, 0, 2))
    keep_scale = linked[length - 1] * jnp.exp(cumulative[length - 1])
    carry_map = keep_scale[:, None, None] * jnp.eye(keyset.shape[2], dtype=jnp.float32)[
        None
    ] - product("hcd,hce->hde", pushed, carried)
    injected = product("hcd,hce->hde", pushed, fresh_part)
    return (local_out, reach_back, carry_map, injected)


def finish(outputs, z_part, norm_gain):
    scale = lax.rsqrt(jnp.mean(outputs * outputs, axis=2, keepdims=True) + 1e-06)
    gating = jax.nn.silu(z_part.astype(jnp.float32).reshape(outputs.shape))
    result = outputs * scale * norm_gain.astype(jnp.float32)[None, None, :] * gating
    return result.astype(jnp.bfloat16).reshape(outputs.shape[0], -1)


MESH = pl.DeviceIdType.MESH


def fold(high, low):
    return jnp.dot(high, low, precision=highest, preferred_element_type=jnp.float32)


def chain_kernel(
    devices, carry_ref, inject_ref, out_ref,
    got1_a, got1_b, got2_a, got2_b, got3_b, got4_b,
    lo_a, lo_b, join_a, join_b, pair_a, pair_b, quad_b, reply,
    send_sems, recv_sems,
):
    me = lax.axis_index("req")
    tp_me = lax.axis_index("tp")
    core = lax.rem(me, 2)
    partner = me + 1 - 2 * core

    def at(device):
        return (lax.rem(device + devices, devices), tp_me)

    barrier = pltpu.get_barrier_semaphore()
    for peer in (partner, me + 2, me - 2, me + 4, me - 4):
        pl.semaphore_signal(barrier, inc=1, device_id=at(peer), device_id_type=MESH)
    pl.semaphore_wait(barrier, 5)

    def remote(step, slot, src, dst, target):
        return pltpu.make_async_remote_copy(
            src_ref=src, dst_ref=dst,
            send_sem=send_sems.at[step, slot], recv_sem=recv_sems.at[step, slot],
            device_id=at(target), device_id_type=MESH,
        )

    def along(step, pairs, shift):
        copies = [remote(step, slot, src, dst, me + shift) for slot, (src, dst) in enumerate(pairs)]

        @pl.when(me + shift < devices)
        def _():
            for copy in copies:
                copy.start()

        @pl.when(me >= shift)
        def _():
            for copy in copies:
                copy.wait_recv()

        @pl.when(me < shift)
        def _():
            for _, dst in pairs:
                dst[...] = jnp.zeros(dst.shape, dst.dtype)

        return copies

    def sent(copies, shift):
        @pl.when(me + shift < devices)
        def _():
            for copy in copies:
                copy.wait_send()

    first = [
        remote(0, 0, carry_ref.at[1 - core], got1_a, partner),
        remote(0, 1, inject_ref.at[1 - core], got1_b, partner),
    ]
    for copy in first:
        copy.start()
    for copy in first:
        copy.wait_recv()
    own_a = carry_ref[core]
    own_b = inject_ref[core]
    low = core == 0
    lo_a[...] = jnp.where(low, own_a, got1_a[...])
    lo_b[...] = jnp.where(low, own_b, got1_b[...])
    hi_a = jnp.where(low, got1_a[...], own_a)
    hi_b = jnp.where(low, got1_b[...], own_b)
    join_a[...] = fold(hi_a, lo_a[...])
    join_b[...] = fold(hi_a, lo_b[...]) + hi_b
    for copy in first:
        copy.wait_send()

    copies = along(1, ((join_a, got2_a), (join_b, got2_b)), 2)
    pair_a[...] = fold(join_a[...], got2_a[...])
    pair_b[...] = fold(join_a[...], got2_b[...]) + join_b[...]
    sent(copies, 2)

    copies = along(2, ((pair_b, got3_b),), 4)
    quad_b[...] = fold(pair_a[...], got3_b[...]) + pair_b[...]
    sent(copies, 4)

    copies = along(3, ((quad_b, got4_b),), 2)
    entering = got4_b[...]
    onward = fold(lo_a[...], entering) + lo_b[...]
    sent(copies, 2)

    reply[...] = jnp.where(low, onward, entering)
    last = remote(4, 0, reply, out_ref.at[core], partner)
    last.start()
    out_ref[core] = jnp.where(low, entering, onward)
    remote(4, 0, reply, out_ref.at[1 - core], partner).wait_recv()
    last.wait_send()


def carried_in(carry_total, inject_total, devices):
    heads, dk, dv = inject_total.shape
    a_shape = pltpu.VMEM((dk, dk), jnp.float32)
    b_shape = pltpu.VMEM((dk, dv), jnp.float32)
    return pl.pallas_call(
        functools.partial(chain_kernel, devices),
        out_shape=jax.ShapeDtypeStruct((heads, dk, dv), jnp.float32),
        in_specs=[pl.BlockSpec(memory_space=pltpu.VMEM)] * 2,
        out_specs=pl.BlockSpec(memory_space=pltpu.VMEM),
        scratch_shapes=[
            a_shape, b_shape, a_shape, b_shape, b_shape, b_shape,
            a_shape, b_shape, a_shape, b_shape, a_shape, b_shape, b_shape, b_shape,
            pltpu.SemaphoreType.DMA((5, 2)),
            pltpu.SemaphoreType.DMA((5, 2)),
        ],
        compiler_params=pltpu.CompilerParams(collective_id=0, has_side_effects=True),
    )(carry_total, inject_total)


def solve_kernel(coupling_ref, rhs_ref, out_ref):
    length = coupling_ref.shape[1]
    rows = lax.broadcasted_iota(jnp.int32, (length, length), 0)
    cols = lax.broadcasted_iota(jnp.int32, (length, length), 1)
    eye = (rows == cols).astype(jnp.float32)
    for h in range(coupling_ref.shape[0]):
        power = -coupling_ref[h]
        inverse = eye + power
        span = 2
        while span < length:
            power = fold(power, power)
            inverse = inverse + fold(inverse, power)
            span *= 2
        out_ref[h] = fold(inverse, rhs_ref[h])


def unit_lower_solve(coupling, rhs):
    return pl.pallas_call(
        solve_kernel,
        out_shape=jax.ShapeDtypeStruct(rhs.shape, jnp.float32),
        in_specs=[pl.BlockSpec(memory_space=pltpu.VMEM)] * 2,
        out_specs=pl.BlockSpec(memory_space=pltpu.VMEM),
    )(coupling, rhs)


def local(
    layer_input,
    q_in,
    k_in,
    v_in,
    z_in,
    conv_q,
    conv_k,
    conv_v,
    gate_weight,
    decay_rate,
    dt_bias,
    norm_gain,
    segment_ids,
):
    row_count = q_in.shape[0]
    local_heads = q_in.shape[1] // DK
    edge_rows = CONV - 1
    seg_marks = (segment_ids[row_count - edge_rows :] + 1).astype(jnp.bfloat16)[:, None]
    q_width, k_width = q_in.shape[1], k_in.shape[1]
    edges = jnp.concatenate(
        [
            q_in[row_count - edge_rows :],
            k_in[row_count - edge_rows :],
            v_in[row_count - edge_rows :],
            seg_marks,
        ],
        axis=1,
    )
    prior = passed_along(edges, "req", 1)
    prior_q = prior[:, :q_width]
    prior_k = prior[:, q_width : q_width + k_width]
    prior_v = prior[:, q_width + k_width : -1]
    prior_seg = prior[:, -1].astype(jnp.int32) - 1
    seg_ext = jnp.concatenate([prior_seg, segment_ids])
    queries = short_conv(
        jnp.concatenate([prior_q, q_in]).astype(jnp.float32), seg_ext, conv_q, row_count
    )
    keyset = unit_keys(
        short_conv(
            jnp.concatenate([prior_k, k_in]).astype(jnp.float32), seg_ext, conv_k, row_count
        ),
        local_heads,
    )
    values = short_conv(
        jnp.concatenate([prior_v, v_in]).astype(jnp.float32), seg_ext, conv_v, row_count
    )
    partial_value = jnp.dot(layer_input, gate_weight, preferred_element_type=jnp.float32)
    gate_total = lax.psum(partial_value, "tp")
    head_start = lax.axis_index("tp") * local_heads
    decay_in = lax.dynamic_slice_in_dim(gate_total, head_start, local_heads, 1)
    beta_in = lax.dynamic_slice_in_dim(gate_total, HEADS + head_start, local_heads, 1)
    log_alpha = -decay_rate[None, :] * jax.nn.softplus(decay_in + dt_bias[None, :])
    beta_gate = jax.nn.sigmoid(beta_in)
    local_out, reach_back, carry_map, injected = block_terms(
        queries.reshape(row_count, local_heads, DK),
        keyset,
        values.reshape(row_count, local_heads, DV),
        log_alpha,
        beta_gate,
        segment_ids,
        prior_seg[edge_rows - 1],
    )
    incoming = carried_in(carry_map, injected, lax.axis_size("req"))
    head_out = local_out + product("hcd,hde->hce", reach_back, incoming)
    head_out = jnp.transpose(head_out, (1, 0, 2))
    return finish(head_out, z_in, norm_gain)


def solution(mesh):
    placed = (
        P("req", "tp"),
        P("req", "tp"),
        P("req", "tp"),
        P("req", "tp"),
        P("req", "tp"),
        P(None, "tp"),
        P(None, "tp"),
        P(None, "tp"),
        P("tp", None),
        P("tp"),
        P("tp"),
        P(),
        P("req"),
    )
    return jax.shard_map(
        local, mesh=mesh, in_specs=placed, out_specs=P("req", "tp"), check_vma=False
    )
```

```python
import functools

import jax
import jax.numpy as jnp
from jax import lax
from jax.experimental import pallas as pl
from jax.experimental.pallas import tpu as pltpu
from jax.sharding import PartitionSpec as P

HEADS = 8
DK = 128
DV = 256
CONV = 4
BLOCK = 64


highest = lax.Precision.HIGHEST


def passed_along(value, axis, by):
    devices = lax.axis_size(axis)
    pairs = [(i, i + by) for i in range(devices) if 0 <= i + by < devices]
    return lax.ppermute(value, axis, pairs)


def product(pattern, first_op, second_op):
    return jnp.einsum(pattern, first_op, second_op, precision=highest)


def short_conv(extended, seg_ext, weight, row_count):
    own_seg = seg_ext[CONV - 1 :]
    summed = jnp.zeros((row_count, extended.shape[1]), jnp.float32)
    for offset in range(CONV):
        same_req = (seg_ext[offset : offset + row_count] == own_seg)[:, None]
        summed = summed + jnp.where(same_req, extended[offset : offset + row_count], 0.0) * weight[
            offset
        ].astype(jnp.float32)
    return jax.nn.silu(summed)


def unit_keys(key_raw, heads):
    shaped = key_raw.reshape(key_raw.shape[0], heads, DK)
    return shaped * lax.rsqrt(jnp.sum(shaped * shaped, axis=2, keepdims=True) + 1e-06)


def block_terms(queries, keyset, values, log_alpha, beta_gate, seg_block, seg_before):
    length = seg_block.shape[0]
    width = values.shape[2]
    cumulative = jnp.cumsum(log_alpha, axis=0)
    positions = jnp.arange(length)
    same_req = seg_block[:, None] == seg_block[None, :]
    causal = (positions[:, None] >= positions[None, :]) & same_req
    strict = (positions[:, None] > positions[None, :]) & same_req
    gap_log = jnp.transpose(cumulative[:, None, :] - cumulative[None, :, :], (2, 0, 1))
    decays = jnp.where(causal[None], jnp.exp(jnp.where(causal[None], gap_log, 0.0)), 0.0)
    linked = (seg_block == seg_before).astype(jnp.float32)
    tail_mask = (seg_block == seg_block[length - 1]).astype(jnp.float32)
    key_dots = product("ihd,jhd->hij", keyset, keyset)
    coupling = (
        jnp.transpose(beta_gate)[:, :, None] * key_dots * jnp.where(strict[None], decays, 0.0)
    )
    start_scale = jnp.exp(cumulative) * linked[:, None]
    right_side = jnp.concatenate(
        [beta_gate[:, :, None] * values, (beta_gate * start_scale)[:, :, None] * keyset], axis=2
    )
    solved = unit_lower_solve(coupling, jnp.transpose(right_side, (1, 0, 2)))
    fresh_part = solved[:, :, :width]
    carried = solved[:, :, width:]
    scores = product("ihd,jhd->hij", queries, keyset) * decays
    reach_back = jnp.transpose(queries * start_scale[:, :, None], (1, 0, 2)) - product(
        "hij,hjd->hid", scores, carried
    )
    local_out = product("hij,hjd->hid", scores, fresh_part)
    fade_out = jnp.exp(cumulative[length - 1][None, :] - cumulative) * tail_mask[:, None]
    pushed = jnp.transpose(fade_out[:, :, None] * keyset, (1, 0, 2))
    keep_scale = linked[length - 1] * jnp.exp(cumulative[length - 1])
    carry_map = keep_scale[:, None, None] * jnp.eye(keyset.shape[2], dtype=jnp.float32)[
        None
    ] - product("hcd,hce->hde", pushed, carried)
    injected = product("hcd,hce->hde", pushed, fresh_part)
    return (local_out, reach_back, carry_map, injected)


def finish(outputs, z_part, norm_gain):
    scale = lax.rsqrt(jnp.mean(outputs * outputs, axis=2, keepdims=True) + 1e-06)
    gating = jax.nn.silu(z_part.astype(jnp.float32).reshape(outputs.shape))
    result = outputs * scale * norm_gain.astype(jnp.float32)[None, None, :] * gating
    return result.astype(jnp.bfloat16).reshape(outputs.shape[0], -1)


MESH = pl.DeviceIdType.MESH


def fold(high, low):
    return jnp.dot(high, low, precision=highest, preferred_element_type=jnp.float32)


def chain_kernel(
    devices, carry_ref, inject_ref, out_ref,
    got1_a, got1_b, got2_a, got2_b, got3_b, got4_b,
    lo_a, lo_b, join_a, join_b, pair_a, pair_b, quad_b, reply,
    send_sems, recv_sems,
):
    me = lax.axis_index("req")
    tp_me = lax.axis_index("tp")
    core = lax.rem(me, 2)
    partner = me + 1 - 2 * core

    def at(device):
        return (lax.rem(device + devices, devices), tp_me)

    barrier = pltpu.get_barrier_semaphore()
    for peer in (partner, me + 2, me - 2, me + 4, me - 4):
        pl.semaphore_signal(barrier, inc=1, device_id=at(peer), device_id_type=MESH)
    pl.semaphore_wait(barrier, 5)

    def remote(step, slot, src, dst, target):
        return pltpu.make_async_remote_copy(
            src_ref=src, dst_ref=dst,
            send_sem=send_sems.at[step, slot], recv_sem=recv_sems.at[step, slot],
            device_id=at(target), device_id_type=MESH,
        )

    def along(step, pairs, shift):
        copies = [remote(step, slot, src, dst, me + shift) for slot, (src, dst) in enumerate(pairs)]

        @pl.when(me + shift < devices)
        def _():
            for copy in copies:
                copy.start()

        @pl.when(me >= shift)
        def _():
            for copy in copies:
                copy.wait_recv()

        @pl.when(me < shift)
        def _():
            for _, dst in pairs:
                dst[...] = jnp.zeros(dst.shape, dst.dtype)

        return copies

    def sent(copies, shift):
        @pl.when(me + shift < devices)
        def _():
            for copy in copies:
                copy.wait_send()

    first = [
        remote(0, 0, carry_ref.at[1 - core], got1_a, partner),
        remote(0, 1, inject_ref.at[1 - core], got1_b, partner),
    ]
    for copy in first:
        copy.start()
    for copy in first:
        copy.wait_recv()
    own_a = carry_ref[core]
    own_b = inject_ref[core]
    low = core == 0
    lo_a[...] = jnp.where(low, own_a, got1_a[...])
    lo_b[...] = jnp.where(low, own_b, got1_b[...])
    hi_a = jnp.where(low, got1_a[...], own_a)
    hi_b = jnp.where(low, got1_b[...], own_b)
    join_a[...] = fold(hi_a, lo_a[...])
    join_b[...] = fold(hi_a, lo_b[...]) + hi_b
    for copy in first:
        copy.wait_send()

    copies = along(1, ((join_a, got2_a), (join_b, got2_b)), 2)
    pair_a[...] = fold(join_a[...], got2_a[...])
    pair_b[...] = fold(join_a[...], got2_b[...]) + join_b[...]
    sent(copies, 2)

    copies = along(2, ((pair_b, got3_b),), 4)
    quad_b[...] = fold(pair_a[...], got3_b[...]) + pair_b[...]
    sent(copies, 4)

    copies = along(3, ((quad_b, got4_b),), 2)
    entering = got4_b[...]
    onward = fold(lo_a[...], entering) + lo_b[...]
    sent(copies, 2)

    reply[...] = jnp.where(low, onward, entering)
    last = remote(4, 0, reply, out_ref.at[core], partner)
    last.start()
    out_ref[core] = jnp.where(low, entering, onward)
    remote(4, 0, reply, out_ref.at[1 - core], partner).wait_recv()
    last.wait_send()


def carried_in(carry_total, inject_total, devices):
    heads, dk, dv = inject_total.shape
    a_shape = pltpu.VMEM((dk, dk), jnp.float32)
    b_shape = pltpu.VMEM((dk, dv), jnp.float32)
    return pl.pallas_call(
        functools.partial(chain_kernel, devices),
        out_shape=jax.ShapeDtypeStruct((heads, dk, dv), jnp.float32),
        in_specs=[pl.BlockSpec(memory_space=pltpu.VMEM)] * 2,
        out_specs=pl.BlockSpec(memory_space=pltpu.VMEM),
        scratch_shapes=[
            a_shape, b_shape, a_shape, b_shape, b_shape, b_shape,
            a_shape, b_shape, a_shape, b_shape, a_shape, b_shape, b_shape, b_shape,
            pltpu.SemaphoreType.DMA((5, 2)),
            pltpu.SemaphoreType.DMA((5, 2)),
        ],
        compiler_params=pltpu.CompilerParams(collective_id=0, has_side_effects=True),
    )(carry_total, inject_total)


def solve_kernel(coupling_ref, rhs_ref, out_ref):
    length = coupling_ref.shape[1]
    rows = lax.broadcasted_iota(jnp.int32, (length, length), 0)
    cols = lax.broadcasted_iota(jnp.int32, (length, length), 1)
    eye = (rows == cols).astype(jnp.float32)
    for h in range(coupling_ref.shape[0]):
        power = -coupling_ref[h]
        inverse = eye + power
        span = 2
        while span < length:
            power = fold(power, power)
            inverse = inverse + fold(inverse, power)
            span *= 2
        out_ref[h] = fold(inverse, rhs_ref[h])


def unit_lower_solve(coupling, rhs):
    return pl.pallas_call(
        solve_kernel,
        out_shape=jax.ShapeDtypeStruct(rhs.shape, jnp.float32),
        in_specs=[pl.BlockSpec(memory_space=pltpu.VMEM)] * 2,
        out_specs=pl.BlockSpec(memory_space=pltpu.VMEM),
    )(coupling, rhs)


def gate_kernel(groups, input_ref, weight_ref, out_ref, partial, got, send_sems, recv_sems):
    me = lax.axis_index("tp")
    row = lax.axis_index("req")
    barrier = pltpu.get_barrier_semaphore()
    for step in range(1, groups):
        pl.semaphore_signal(
            barrier, inc=1, device_id=(row, lax.rem(me + step, groups)), device_id_type=MESH
        )
    pl.semaphore_wait(barrier, groups - 1)
    partial[...] = jnp.dot(input_ref[...], weight_ref[...], preferred_element_type=jnp.float32)
    copies = []
    for step in range(1, groups):
        copies.append(
            pltpu.make_async_remote_copy(
                src_ref=partial,
                dst_ref=got.at[me],
                send_sem=send_sems.at[step],
                recv_sem=recv_sems.at[me],
                device_id=(row, lax.rem(me + step, groups)),
                device_id_type=MESH,
            )
        )
    for copy in copies:
        copy.start()
    for source in range(groups):

        @pl.when(source != me)
        def _():
            pltpu.make_async_remote_copy(
                src_ref=partial,
                dst_ref=got.at[source],
                send_sem=send_sems.at[0],
                recv_sem=recv_sems.at[source],
                device_id=(row, source),
                device_id_type=MESH,
            ).wait_recv()

    total = jnp.zeros(out_ref.shape, jnp.float32)
    for source in range(groups):
        total = total + jnp.where(source == me, partial[...], got[source])
    out_ref[...] = total
    for copy in copies:
        copy.wait_send()


def gate_sum(layer_input, gate_weight, groups):
    rows, width = layer_input.shape[0], gate_weight.shape[1]
    return pl.pallas_call(
        functools.partial(gate_kernel, groups),
        out_shape=jax.ShapeDtypeStruct((rows, width), jnp.float32),
        in_specs=[pl.BlockSpec(memory_space=pltpu.VMEM)] * 2,
        out_specs=pl.BlockSpec(memory_space=pltpu.VMEM),
        scratch_shapes=[
            pltpu.VMEM((rows, width), jnp.float32),
            pltpu.VMEM((groups, rows, width), jnp.float32),
            pltpu.SemaphoreType.DMA((groups,)),
            pltpu.SemaphoreType.DMA((groups,)),
        ],
        compiler_params=pltpu.CompilerParams(collective_id=1, has_side_effects=True),
    )(layer_input, gate_weight)


def local(
    layer_input,
    q_in,
    k_in,
    v_in,
    z_in,
    conv_q,
    conv_k,
    conv_v,
    gate_weight,
    decay_rate,
    dt_bias,
    norm_gain,
    segment_ids,
):
    row_count = q_in.shape[0]
    local_heads = q_in.shape[1] // DK
    edge_rows = CONV - 1
    seg_marks = (segment_ids[row_count - edge_rows :] + 1).astype(jnp.bfloat16)[:, None]
    q_width, k_width = q_in.shape[1], k_in.shape[1]
    edges = jnp.concatenate(
        [
            q_in[row_count - edge_rows :],
            k_in[row_count - edge_rows :],
            v_in[row_count - edge_rows :],
            seg_marks,
        ],
        axis=1,
    )
    prior = passed_along(edges, "req", 1)
    prior_q = prior[:, :q_width]
    prior_k = prior[:, q_width : q_width + k_width]
    prior_v = prior[:, q_width + k_width : -1]
    prior_seg = prior[:, -1].astype(jnp.int32) - 1
    seg_ext = jnp.concatenate([prior_seg, segment_ids])
    queries = short_conv(
        jnp.concatenate([prior_q, q_in]).astype(jnp.float32), seg_ext, conv_q, row_count
    )
    keyset = unit_keys(
        short_conv(
            jnp.concatenate([prior_k, k_in]).astype(jnp.float32), seg_ext, conv_k, row_count
        ),
        local_heads,
    )
    values = short_conv(
        jnp.concatenate([prior_v, v_in]).astype(jnp.float32), seg_ext, conv_v, row_count
    )
    gate_total = gate_sum(layer_input, gate_weight, lax.axis_size("tp"))
    head_start = lax.axis_index("tp") * local_heads
    decay_in = lax.dynamic_slice_in_dim(gate_total, head_start, local_heads, 1)
    beta_in = lax.dynamic_slice_in_dim(gate_total, HEADS + head_start, local_heads, 1)
    log_alpha = -decay_rate[None, :] * jax.nn.softplus(decay_in + dt_bias[None, :])
    beta_gate = jax.nn.sigmoid(beta_in)
    local_out, reach_back, carry_map, injected = block_terms(
        queries.reshape(row_count, local_heads, DK),
        keyset,
        values.reshape(row_count, local_heads, DV),
        log_alpha,
        beta_gate,
        segment_ids,
        prior_seg[edge_rows - 1],
    )
    incoming = carried_in(carry_map, injected, lax.axis_size("req"))
    head_out = local_out + product("hcd,hde->hce", reach_back, incoming)
    head_out = jnp.transpose(head_out, (1, 0, 2))
    return finish(head_out, z_in, norm_gain)


def solution(mesh):
    placed = (
        P("req", "tp"),
        P("req", "tp"),
        P("req", "tp"),
        P("req", "tp"),
        P("req", "tp"),
        P(None, "tp"),
        P(None, "tp"),
        P(None, "tp"),
        P("tp", None),
        P("tp"),
        P("tp"),
        P(),
        P("req"),
    )
    return jax.shard_map(
        local, mesh=mesh, in_specs=placed, out_specs=P("req", "tp"), check_vma=False
    )
```

```python
import functools

import jax
import jax.numpy as jnp
from jax import lax
from jax.experimental import pallas as pl
from jax.experimental.pallas import tpu as pltpu
from jax.sharding import PartitionSpec as P

HEADS = 8
DK = 128
DV = 256
CONV = 4
BLOCK = 64


highest = lax.Precision.HIGHEST


def passed_along(value, axis, by):
    devices = lax.axis_size(axis)
    pairs = [(i, i + by) for i in range(devices) if 0 <= i + by < devices]
    return lax.ppermute(value, axis, pairs)


def product(pattern, first_op, second_op):
    return jnp.einsum(pattern, first_op, second_op, precision=highest)


def short_conv(extended, seg_ext, weight, row_count):
    own_seg = seg_ext[CONV - 1 :]
    summed = jnp.zeros((row_count, extended.shape[1]), jnp.float32)
    for offset in range(CONV):
        same_req = (seg_ext[offset : offset + row_count] == own_seg)[:, None]
        summed = summed + jnp.where(same_req, extended[offset : offset + row_count], 0.0) * weight[
            offset
        ].astype(jnp.float32)
    return jax.nn.silu(summed)


def unit_keys(key_raw, heads):
    shaped = key_raw.reshape(key_raw.shape[0], heads, DK)
    return shaped * lax.rsqrt(jnp.sum(shaped * shaped, axis=2, keepdims=True) + 1e-06)


def block_terms(queries, keyset, values, log_alpha, beta_gate, seg_block, seg_before):
    length = seg_block.shape[0]
    width = values.shape[2]
    cumulative = jnp.cumsum(log_alpha, axis=0)
    positions = jnp.arange(length)
    same_req = seg_block[:, None] == seg_block[None, :]
    causal = (positions[:, None] >= positions[None, :]) & same_req
    strict = (positions[:, None] > positions[None, :]) & same_req
    gap_log = jnp.transpose(cumulative[:, None, :] - cumulative[None, :, :], (2, 0, 1))
    decays = jnp.where(causal[None], jnp.exp(jnp.where(causal[None], gap_log, 0.0)), 0.0)
    linked = (seg_block == seg_before).astype(jnp.float32)
    tail_mask = (seg_block == seg_block[length - 1]).astype(jnp.float32)
    key_dots = product("ihd,jhd->hij", keyset, keyset)
    coupling = (
        jnp.transpose(beta_gate)[:, :, None] * key_dots * jnp.where(strict[None], decays, 0.0)
    )
    start_scale = jnp.exp(cumulative) * linked[:, None]
    right_side = jnp.concatenate(
        [beta_gate[:, :, None] * values, (beta_gate * start_scale)[:, :, None] * keyset], axis=2
    )
    solved = unit_lower_solve(coupling, jnp.transpose(right_side, (1, 0, 2)))
    fresh_part = solved[:, :, :width]
    carried = solved[:, :, width:]
    scores = product("ihd,jhd->hij", queries, keyset) * decays
    reach_back = jnp.transpose(queries * start_scale[:, :, None], (1, 0, 2)) - product(
        "hij,hjd->hid", scores, carried
    )
    local_out = product("hij,hjd->hid", scores, fresh_part)
    fade_out = jnp.exp(cumulative[length - 1][None, :] - cumulative) * tail_mask[:, None]
    pushed = jnp.transpose(fade_out[:, :, None] * keyset, (1, 0, 2))
    keep_scale = linked[length - 1] * jnp.exp(cumulative[length - 1])
    carry_map = keep_scale[:, None, None] * jnp.eye(keyset.shape[2], dtype=jnp.float32)[
        None
    ] - product("hcd,hce->hde", pushed, carried)
    injected = product("hcd,hce->hde", pushed, fresh_part)
    return (local_out, reach_back, carry_map, injected)


def finish(outputs, z_part, norm_gain):
    scale = lax.rsqrt(jnp.mean(outputs * outputs, axis=2, keepdims=True) + 1e-06)
    gating = jax.nn.silu(z_part.astype(jnp.float32).reshape(outputs.shape))
    result = outputs * scale * norm_gain.astype(jnp.float32)[None, None, :] * gating
    return result.astype(jnp.bfloat16).reshape(outputs.shape[0], -1)


MESH = pl.DeviceIdType.MESH


def fold(high, low):
    return jnp.dot(high, low, precision=highest, preferred_element_type=jnp.float32)


def chain_kernel(
    devices, carry_ref, inject_ref, out_ref,
    got1_a, got1_b, got2_a, got2_b, got3_b, got4_b,
    lo_a, lo_b, join_a, join_b, pair_a, pair_b, quad_b, reply,
    send_sems, recv_sems,
):
    me = lax.axis_index("req")
    tp_me = lax.axis_index("tp")
    core = lax.rem(me, 2)
    partner = me + 1 - 2 * core

    def at(device):
        return (lax.rem(device + devices, devices), tp_me)

    barrier = pltpu.get_barrier_semaphore()
    for peer in (partner, me + 2, me - 2, me + 4, me - 4):
        pl.semaphore_signal(barrier, inc=1, device_id=at(peer), device_id_type=MESH)
    pl.semaphore_wait(barrier, 5)

    def remote(step, slot, src, dst, target):
        return pltpu.make_async_remote_copy(
            src_ref=src, dst_ref=dst,
            send_sem=send_sems.at[step, slot], recv_sem=recv_sems.at[step, slot],
            device_id=at(target), device_id_type=MESH,
        )

    def along(step, pairs, shift):
        copies = [remote(step, slot, src, dst, me + shift) for slot, (src, dst) in enumerate(pairs)]

        @pl.when(me + shift < devices)
        def _():
            for copy in copies:
                copy.start()

        @pl.when(me >= shift)
        def _():
            for copy in copies:
                copy.wait_recv()

        @pl.when(me < shift)
        def _():
            for _, dst in pairs:
                dst[...] = jnp.zeros(dst.shape, dst.dtype)

        return copies

    def sent(copies, shift):
        @pl.when(me + shift < devices)
        def _():
            for copy in copies:
                copy.wait_send()

    first = [
        remote(0, 0, carry_ref.at[1 - core], got1_a, partner),
        remote(0, 1, inject_ref.at[1 - core], got1_b, partner),
    ]
    for copy in first:
        copy.start()
    for copy in first:
        copy.wait_recv()
    own_a = carry_ref[core]
    own_b = inject_ref[core]
    low = core == 0
    lo_a[...] = jnp.where(low, own_a, got1_a[...])
    lo_b[...] = jnp.where(low, own_b, got1_b[...])
    hi_a = jnp.where(low, got1_a[...], own_a)
    hi_b = jnp.where(low, got1_b[...], own_b)
    join_a[...] = fold(hi_a, lo_a[...])
    join_b[...] = fold(hi_a, lo_b[...]) + hi_b
    for copy in first:
        copy.wait_send()

    copies = along(1, ((join_a, got2_a), (join_b, got2_b)), 2)
    pair_a[...] = fold(join_a[...], got2_a[...])
    pair_b[...] = fold(join_a[...], got2_b[...]) + join_b[...]
    sent(copies, 2)

    copies = along(2, ((pair_b, got3_b),), 4)
    quad_b[...] = fold(pair_a[...], got3_b[...]) + pair_b[...]
    sent(copies, 4)

    copies = along(3, ((quad_b, got4_b),), 2)
    entering = got4_b[...]
    onward = fold(lo_a[...], entering) + lo_b[...]
    sent(copies, 2)

    reply[...] = jnp.where(low, onward, entering)
    last = remote(4, 0, reply, out_ref.at[core], partner)
    last.start()
    out_ref[core] = jnp.where(low, entering, onward)
    remote(4, 0, reply, out_ref.at[1 - core], partner).wait_recv()
    last.wait_send()


def carried_in(carry_total, inject_total, devices):
    heads, dk, dv = inject_total.shape
    a_shape = pltpu.VMEM((dk, dk), jnp.float32)
    b_shape = pltpu.VMEM((dk, dv), jnp.float32)
    return pl.pallas_call(
        functools.partial(chain_kernel, devices),
        out_shape=jax.ShapeDtypeStruct((heads, dk, dv), jnp.float32),
        in_specs=[pl.BlockSpec(memory_space=pltpu.VMEM)] * 2,
        out_specs=pl.BlockSpec(memory_space=pltpu.VMEM),
        scratch_shapes=[
            a_shape, b_shape, a_shape, b_shape, b_shape, b_shape,
            a_shape, b_shape, a_shape, b_shape, a_shape, b_shape, b_shape, b_shape,
            pltpu.SemaphoreType.DMA((5, 2)),
            pltpu.SemaphoreType.DMA((5, 2)),
        ],
        compiler_params=pltpu.CompilerParams(collective_id=0, has_side_effects=True),
    )(carry_total, inject_total)


def solve_kernel(coupling_ref, rhs_ref, out_ref):
    length = coupling_ref.shape[1]
    rows = lax.broadcasted_iota(jnp.int32, (length, length), 0)
    cols = lax.broadcasted_iota(jnp.int32, (length, length), 1)
    eye = (rows == cols).astype(jnp.float32)
    for h in range(coupling_ref.shape[0]):
        power = -coupling_ref[h]
        inverse = eye + power
        span = 2
        while span < length:
            power = fold(power, power)
            inverse = inverse + fold(inverse, power)
            span *= 2
        out_ref[h] = fold(inverse, rhs_ref[h])


def unit_lower_solve(coupling, rhs):
    return pl.pallas_call(
        solve_kernel,
        out_shape=jax.ShapeDtypeStruct(rhs.shape, jnp.float32),
        in_specs=[pl.BlockSpec(memory_space=pltpu.VMEM)] * 2,
        out_specs=pl.BlockSpec(memory_space=pltpu.VMEM),
    )(coupling, rhs)


def gate_kernel(groups, input_ref, weight_ref, out_ref, partial, got, send_sems, recv_sems):
    me = lax.axis_index("tp")
    row = lax.axis_index("req")
    barrier = pltpu.get_barrier_semaphore()
    for step in range(1, groups):
        pl.semaphore_signal(
            barrier, inc=1, device_id=(row, lax.rem(me + step, groups)), device_id_type=MESH
        )
    pl.semaphore_wait(barrier, groups - 1)
    partial[...] = jnp.dot(input_ref[...], weight_ref[...], preferred_element_type=jnp.float32)
    copies = []
    for step in range(1, groups):
        copies.append(
            pltpu.make_async_remote_copy(
                src_ref=partial,
                dst_ref=got.at[me],
                send_sem=send_sems.at[step],
                recv_sem=recv_sems.at[me],
                device_id=(row, lax.rem(me + step, groups)),
                device_id_type=MESH,
            )
        )
    for copy in copies:
        copy.start()
    for source in range(groups):

        @pl.when(source != me)
        def _():
            pltpu.make_async_remote_copy(
                src_ref=partial,
                dst_ref=got.at[source],
                send_sem=send_sems.at[0],
                recv_sem=recv_sems.at[source],
                device_id=(row, source),
                device_id_type=MESH,
            ).wait_recv()

    total = jnp.zeros(out_ref.shape, jnp.float32)
    for source in range(groups):
        total = total + jnp.where(source == me, partial[...], got[source])
    out_ref[...] = total
    for copy in copies:
        copy.wait_send()


def gate_sum(layer_input, gate_weight, groups):
    rows, width = layer_input.shape[0], gate_weight.shape[1]
    return pl.pallas_call(
        functools.partial(gate_kernel, groups),
        out_shape=jax.ShapeDtypeStruct((rows, width), jnp.float32),
        in_specs=[pl.BlockSpec(memory_space=pltpu.VMEM)] * 2,
        out_specs=pl.BlockSpec(memory_space=pltpu.VMEM),
        scratch_shapes=[
            pltpu.VMEM((rows, width), jnp.float32),
            pltpu.VMEM((groups, rows, width), jnp.float32),
            pltpu.SemaphoreType.DMA((groups,)),
            pltpu.SemaphoreType.DMA((groups,)),
        ],
        compiler_params=pltpu.CompilerParams(collective_id=1, has_side_effects=True),
    )(layer_input, gate_weight)


def fold_t(left, right):
    return lax.dot_general(
        left, right, (((1,), (1,)), ((), ())), precision=highest,
        preferred_element_type=jnp.float32,
    )


def inverse_unit_lower(coupling, eye):
    length = coupling.shape[0]
    power = -coupling
    inverse = eye + power
    span = 2
    while span < length:
        power = fold(power, power)
        inverse = inverse + fold(inverse, power)
        span *= 2
    return inverse


def chunk_kernel(
    ext_ref, seg_ref, taps_ref, gates_ref,
    local_ref, reach_ref, carry_ref, inject_ref,
):
    length = local_ref.shape[1]
    heads = local_ref.shape[0]
    dk = carry_ref.shape[1]
    dv = local_ref.shape[2]
    edge = ext_ref.shape[0] - length
    q_end = heads * dk
    k_end = 2 * heads * dk

    own_seg = seg_ref[pl.ds(edge, length), :]
    summed = None
    for offset in range(edge + 1):
        term = jnp.where(
            seg_ref[pl.ds(offset, length), :] == own_seg,
            ext_ref[pl.ds(offset, length), :],
            0.0,
        ) * taps_ref[pl.ds(offset, 1), :]
        summed = term if summed is None else summed + term
    mixed_in = summed / (1.0 + jnp.exp(-summed))

    rows = lax.broadcasted_iota(jnp.int32, (length, length), 0)
    cols = lax.broadcasted_iota(jnp.int32, (length, length), 1)
    eye = (rows == cols).astype(jnp.float32)
    lower_ones = (rows >= cols).astype(jnp.float32)
    seg_grid = jnp.broadcast_to(own_seg, (length, length))
    same = seg_grid == jnp.transpose(seg_grid)
    causal = (rows >= cols) & same
    strict = (rows > cols) & same
    linked = (own_seg == seg_ref[pl.ds(edge - 1, 1), :]).astype(jnp.float32)
    tail = (own_seg == seg_ref[pl.ds(edge + length - 1, 1), :]).astype(jnp.float32)
    linked_last = linked[length - 1 :, :]

    for h in range(heads):
        queries = mixed_in[:, h * dk : (h + 1) * dk]
        key_raw = mixed_in[:, q_end + h * dk : q_end + (h + 1) * dk]
        values = mixed_in[:, k_end + h * dv : k_end + (h + 1) * dv]
        keys = key_raw * lax.rsqrt(jnp.sum(key_raw * key_raw, axis=1, keepdims=True) + 1e-06)
        log_alpha = gates_ref[:, h : h + 1]
        beta = gates_ref[:, heads + h : heads + h + 1]
        cum_grid = fold(lower_ones, jnp.broadcast_to(log_alpha, (length, length)))
        cumulative = cum_grid[:, 0:1]
        last = cum_grid[length - 1 :, 0:1]
        gap = cum_grid - jnp.transpose(cum_grid)
        decays = jnp.where(causal, jnp.exp(jnp.where(causal, gap, 0.0)), 0.0)
        coupling = beta * fold_t(keys, keys) * jnp.where(strict, decays, 0.0)
        inverse = inverse_unit_lower(coupling, eye)
        start_scale = jnp.exp(cumulative) * linked
        fresh = fold(inverse, beta * values)
        carried = fold(inverse, (beta * start_scale) * keys)
        scores = fold_t(queries, keys) * decays
        reach_ref[h] = queries * start_scale - fold(scores, carried)
        local_ref[h] = fold(scores, fresh)
        fade_out = jnp.exp(last - cumulative) * tail
        pushed_t = jnp.transpose(fade_out * keys)
        keep = linked_last * jnp.exp(last)
        carry_ref[h] = keep * eye - fold(pushed_t, carried)
        inject_ref[h] = fold(pushed_t, fresh)


def chunk_terms(ext, seg_ext, taps, gates, heads):
    length = ext.shape[0] - (CONV - 1)
    shapes = (
        jax.ShapeDtypeStruct((heads, length, DV), jnp.float32),
        jax.ShapeDtypeStruct((heads, length, DK), jnp.float32),
        jax.ShapeDtypeStruct((heads, DK, DK), jnp.float32),
        jax.ShapeDtypeStruct((heads, DK, DV), jnp.float32),
    )
    return pl.pallas_call(
        chunk_kernel,
        out_shape=shapes,
        in_specs=[pl.BlockSpec(memory_space=pltpu.VMEM)] * 4,
        out_specs=[pl.BlockSpec(memory_space=pltpu.VMEM)] * 4,
    )(ext, seg_ext, taps, gates)


def local(
    layer_input,
    q_in,
    k_in,
    v_in,
    z_in,
    conv_q,
    conv_k,
    conv_v,
    gate_weight,
    decay_rate,
    dt_bias,
    norm_gain,
    segment_ids,
):
    row_count = q_in.shape[0]
    local_heads = q_in.shape[1] // DK
    edge_rows = CONV - 1
    seg_marks = (segment_ids[row_count - edge_rows :] + 1).astype(jnp.bfloat16)[:, None]
    q_width, k_width = q_in.shape[1], k_in.shape[1]
    edges = jnp.concatenate(
        [
            q_in[row_count - edge_rows :],
            k_in[row_count - edge_rows :],
            v_in[row_count - edge_rows :],
            seg_marks,
        ],
        axis=1,
    )
    prior = passed_along(edges, "req", 1)
    prior_seg = prior[:, -1:].astype(jnp.float32) - 1.0
    ext = jnp.concatenate(
        [prior[:, :-1], jnp.concatenate([q_in, k_in, v_in], axis=1)], axis=0
    ).astype(jnp.float32)
    seg_ext = jnp.concatenate([prior_seg, segment_ids.astype(jnp.float32)[:, None]], axis=0)
    taps = jnp.concatenate([conv_q, conv_k, conv_v], axis=1).astype(jnp.float32)
    gate_total = gate_sum(layer_input, gate_weight, lax.axis_size("tp"))
    head_start = lax.axis_index("tp") * local_heads
    decay_in = lax.dynamic_slice_in_dim(gate_total, head_start, local_heads, 1)
    beta_in = lax.dynamic_slice_in_dim(gate_total, HEADS + head_start, local_heads, 1)
    log_alpha = -decay_rate[None, :] * jax.nn.softplus(decay_in + dt_bias[None, :])
    beta_gate = jax.nn.sigmoid(beta_in)
    gates = jnp.concatenate([log_alpha, beta_gate], axis=1)
    local_out, reach_back, carry_map, injected = chunk_terms(
        ext, seg_ext, taps, gates, local_heads
    )
    incoming = carried_in(carry_map, injected, lax.axis_size("req"))
    head_out = local_out + product("hcd,hde->hce", reach_back, incoming)
    head_out = jnp.transpose(head_out, (1, 0, 2))
    return finish(head_out, z_in, norm_gain)


def solution(mesh):
    placed = (
        P("req", "tp"),
        P("req", "tp"),
        P("req", "tp"),
        P("req", "tp"),
        P("req", "tp"),
        P(None, "tp"),
        P(None, "tp"),
        P(None, "tp"),
        P("tp", None),
        P("tp"),
        P("tp"),
        P(),
        P("req"),
    )
    return jax.shard_map(
        local, mesh=mesh, in_specs=placed, out_specs=P("req", "tp"), check_vma=False
    )
```

```python
import functools

import jax
import jax.numpy as jnp
from jax import lax
from jax.experimental import pallas as pl
from jax.experimental.pallas import tpu as pltpu
from jax.sharding import PartitionSpec as P

HEADS = 8
DK = 128
DV = 256
CONV = 4
BLOCK = 64


highest = lax.Precision.HIGHEST


def passed_along(value, axis, by):
    devices = lax.axis_size(axis)
    pairs = [(i, i + by) for i in range(devices) if 0 <= i + by < devices]
    return lax.ppermute(value, axis, pairs)


def product(pattern, first_op, second_op):
    return jnp.einsum(pattern, first_op, second_op, precision=highest)


def short_conv(extended, seg_ext, weight, row_count):
    own_seg = seg_ext[CONV - 1 :]
    summed = jnp.zeros((row_count, extended.shape[1]), jnp.float32)
    for offset in range(CONV):
        same_req = (seg_ext[offset : offset + row_count] == own_seg)[:, None]
        summed = summed + jnp.where(same_req, extended[offset : offset + row_count], 0.0) * weight[
            offset
        ].astype(jnp.float32)
    return jax.nn.silu(summed)


def unit_keys(key_raw, heads):
    shaped = key_raw.reshape(key_raw.shape[0], heads, DK)
    return shaped * lax.rsqrt(jnp.sum(shaped * shaped, axis=2, keepdims=True) + 1e-06)


def block_terms(queries, keyset, values, log_alpha, beta_gate, seg_block, seg_before):
    length = seg_block.shape[0]
    width = values.shape[2]
    cumulative = jnp.cumsum(log_alpha, axis=0)
    positions = jnp.arange(length)
    same_req = seg_block[:, None] == seg_block[None, :]
    causal = (positions[:, None] >= positions[None, :]) & same_req
    strict = (positions[:, None] > positions[None, :]) & same_req
    gap_log = jnp.transpose(cumulative[:, None, :] - cumulative[None, :, :], (2, 0, 1))
    decays = jnp.where(causal[None], jnp.exp(jnp.where(causal[None], gap_log, 0.0)), 0.0)
    linked = (seg_block == seg_before).astype(jnp.float32)
    tail_mask = (seg_block == seg_block[length - 1]).astype(jnp.float32)
    key_dots = product("ihd,jhd->hij", keyset, keyset)
    coupling = (
        jnp.transpose(beta_gate)[:, :, None] * key_dots * jnp.where(strict[None], decays, 0.0)
    )
    start_scale = jnp.exp(cumulative) * linked[:, None]
    right_side = jnp.concatenate(
        [beta_gate[:, :, None] * values, (beta_gate * start_scale)[:, :, None] * keyset], axis=2
    )
    solved = unit_lower_solve(coupling, jnp.transpose(right_side, (1, 0, 2)))
    fresh_part = solved[:, :, :width]
    carried = solved[:, :, width:]
    scores = product("ihd,jhd->hij", queries, keyset) * decays
    reach_back = jnp.transpose(queries * start_scale[:, :, None], (1, 0, 2)) - product(
        "hij,hjd->hid", scores, carried
    )
    local_out = product("hij,hjd->hid", scores, fresh_part)
    fade_out = jnp.exp(cumulative[length - 1][None, :] - cumulative) * tail_mask[:, None]
    pushed = jnp.transpose(fade_out[:, :, None] * keyset, (1, 0, 2))
    keep_scale = linked[length - 1] * jnp.exp(cumulative[length - 1])
    carry_map = keep_scale[:, None, None] * jnp.eye(keyset.shape[2], dtype=jnp.float32)[
        None
    ] - product("hcd,hce->hde", pushed, carried)
    injected = product("hcd,hce->hde", pushed, fresh_part)
    return (local_out, reach_back, carry_map, injected)


def finish(outputs, z_part, norm_gain):
    scale = lax.rsqrt(jnp.mean(outputs * outputs, axis=2, keepdims=True) + 1e-06)
    gating = jax.nn.silu(z_part.astype(jnp.float32).reshape(outputs.shape))
    result = outputs * scale * norm_gain.astype(jnp.float32)[None, None, :] * gating
    return result.astype(jnp.bfloat16).reshape(outputs.shape[0], -1)


MESH = pl.DeviceIdType.MESH


def fold(high, low):
    return jnp.dot(high, low, precision=highest, preferred_element_type=jnp.float32)


def chain_kernel(
    devices, carry_ref, inject_ref, out_ref,
    got1_a, got1_b, got2_a, got2_b, got3_b, got4_b,
    lo_a, lo_b, join_a, join_b, pair_a, pair_b, quad_b, reply,
    wire_a, wire_b, wire_pair, wire_quad,
    send_sems, recv_sems,
):
    me = lax.axis_index("req")
    tp_me = lax.axis_index("tp")
    core = lax.rem(me, 2)
    partner = me + 1 - 2 * core

    def at(device):
        return (lax.rem(device + devices, devices), tp_me)

    barrier = pltpu.get_barrier_semaphore()
    for peer in (partner, me + 2, me - 2, me + 4, me - 4):
        pl.semaphore_signal(barrier, inc=1, device_id=at(peer), device_id_type=MESH)
    pl.semaphore_wait(barrier, 5)

    def remote(step, slot, src, dst, target):
        return pltpu.make_async_remote_copy(
            src_ref=src, dst_ref=dst,
            send_sem=send_sems.at[step, slot], recv_sem=recv_sems.at[step, slot],
            device_id=at(target), device_id_type=MESH,
        )

    def along(step, pairs, shift):
        copies = [remote(step, slot, src, dst, me + shift) for slot, (src, dst) in enumerate(pairs)]

        @pl.when(me + shift < devices)
        def _():
            for copy in copies:
                copy.start()

        @pl.when(me >= shift)
        def _():
            for copy in copies:
                copy.wait_recv()

        @pl.when(me < shift)
        def _():
            for _, dst in pairs:
                dst[...] = jnp.zeros(dst.shape, dst.dtype)

        return copies

    def sent(copies, shift):
        @pl.when(me + shift < devices)
        def _():
            for copy in copies:
                copy.wait_send()

    first = [
        remote(0, 0, carry_ref.at[1 - core], got1_a, partner),
        remote(0, 1, inject_ref.at[1 - core], got1_b, partner),
    ]
    for copy in first:
        copy.start()
    for copy in first:
        copy.wait_recv()
    own_a = carry_ref[core]
    own_b = inject_ref[core]
    low = core == 0
    lo_a[...] = jnp.where(low, own_a, got1_a[...])
    lo_b[...] = jnp.where(low, own_b, got1_b[...])
    hi_a = jnp.where(low, got1_a[...], own_a)
    hi_b = jnp.where(low, got1_b[...], own_b)
    join_a[...] = fold(hi_a, lo_a[...])
    join_b[...] = fold(hi_a, lo_b[...]) + hi_b
    wire_a[...] = join_a[...].astype(wire_a.dtype)
    wire_b[...] = join_b[...].astype(wire_b.dtype)
    for copy in first:
        copy.wait_send()

    copies = along(1, ((wire_a, got2_a), (wire_b, got2_b)), 2)
    pair_a[...] = fold(join_a[...], got2_a[...].astype(jnp.float32))
    pair_b[...] = fold(join_a[...], got2_b[...].astype(jnp.float32)) + join_b[...]
    wire_pair[...] = pair_b[...].astype(wire_pair.dtype)
    sent(copies, 2)

    copies = along(2, ((wire_pair, got3_b),), 4)
    quad_b[...] = fold(pair_a[...], got3_b[...].astype(jnp.float32)) + pair_b[...]
    wire_quad[...] = quad_b[...].astype(wire_quad.dtype)
    sent(copies, 4)

    copies = along(3, ((wire_quad, got4_b),), 2)
    entering = got4_b[...].astype(jnp.float32)
    onward = fold(lo_a[...], entering) + lo_b[...]
    sent(copies, 2)

    reply[...] = jnp.where(low, onward, entering)
    last = remote(4, 0, reply, out_ref.at[core], partner)
    last.start()
    out_ref[core] = jnp.where(low, entering, onward)
    remote(4, 0, reply, out_ref.at[1 - core], partner).wait_recv()
    last.wait_send()


def carried_in(carry_total, inject_total, devices):
    heads, dk, dv = inject_total.shape
    a_shape = pltpu.VMEM((dk, dk), jnp.float32)
    b_shape = pltpu.VMEM((dk, dv), jnp.float32)
    a_wire = pltpu.VMEM((dk, dk), jnp.bfloat16)
    b_wire = pltpu.VMEM((dk, dv), jnp.bfloat16)
    return pl.pallas_call(
        functools.partial(chain_kernel, devices),
        out_shape=jax.ShapeDtypeStruct((heads, dk, dv), jnp.float32),
        in_specs=[pl.BlockSpec(memory_space=pltpu.VMEM)] * 2,
        out_specs=pl.BlockSpec(memory_space=pltpu.VMEM),
        scratch_shapes=[
            a_shape, b_shape, a_wire, b_wire, b_wire, b_wire,
            a_shape, b_shape, a_shape, b_shape, a_shape, b_shape, b_shape, b_shape,
            a_wire, b_wire, b_wire, b_wire,
            pltpu.SemaphoreType.DMA((5, 2)),
            pltpu.SemaphoreType.DMA((5, 2)),
        ],
        compiler_params=pltpu.CompilerParams(collective_id=0, has_side_effects=True),
    )(carry_total, inject_total)


def solve_kernel(coupling_ref, rhs_ref, out_ref):
    length = coupling_ref.shape[1]
    rows = lax.broadcasted_iota(jnp.int32, (length, length), 0)
    cols = lax.broadcasted_iota(jnp.int32, (length, length), 1)
    eye = (rows == cols).astype(jnp.float32)
    for h in range(coupling_ref.shape[0]):
        power = -coupling_ref[h]
        inverse = eye + power
        span = 2
        while span < length:
            power = fold(power, power)
            inverse = inverse + fold(inverse, power)
            span *= 2
        out_ref[h] = fold(inverse, rhs_ref[h])


def unit_lower_solve(coupling, rhs):
    return pl.pallas_call(
        solve_kernel,
        out_shape=jax.ShapeDtypeStruct(rhs.shape, jnp.float32),
        in_specs=[pl.BlockSpec(memory_space=pltpu.VMEM)] * 2,
        out_specs=pl.BlockSpec(memory_space=pltpu.VMEM),
    )(coupling, rhs)


def gate_kernel(groups, input_ref, weight_ref, out_ref, partial, got, send_sems, recv_sems):
    me = lax.axis_index("tp")
    row = lax.axis_index("req")
    barrier = pltpu.get_barrier_semaphore()
    for step in range(1, groups):
        pl.semaphore_signal(
            barrier, inc=1, device_id=(row, lax.rem(me + step, groups)), device_id_type=MESH
        )
    pl.semaphore_wait(barrier, groups - 1)
    partial[...] = jnp.dot(input_ref[...], weight_ref[...], preferred_element_type=jnp.float32)
    copies = []
    for step in range(1, groups):
        copies.append(
            pltpu.make_async_remote_copy(
                src_ref=partial,
                dst_ref=got.at[me],
                send_sem=send_sems.at[step],
                recv_sem=recv_sems.at[me],
                device_id=(row, lax.rem(me + step, groups)),
                device_id_type=MESH,
            )
        )
    for copy in copies:
        copy.start()
    for source in range(groups):

        @pl.when(source != me)
        def _():
            pltpu.make_async_remote_copy(
                src_ref=partial,
                dst_ref=got.at[source],
                send_sem=send_sems.at[0],
                recv_sem=recv_sems.at[source],
                device_id=(row, source),
                device_id_type=MESH,
            ).wait_recv()

    total = jnp.zeros(out_ref.shape, jnp.float32)
    for source in range(groups):
        total = total + jnp.where(source == me, partial[...], got[source])
    out_ref[...] = total
    for copy in copies:
        copy.wait_send()


def gate_sum(layer_input, gate_weight, groups):
    rows, width = layer_input.shape[0], gate_weight.shape[1]
    return pl.pallas_call(
        functools.partial(gate_kernel, groups),
        out_shape=jax.ShapeDtypeStruct((rows, width), jnp.float32),
        in_specs=[pl.BlockSpec(memory_space=pltpu.VMEM)] * 2,
        out_specs=pl.BlockSpec(memory_space=pltpu.VMEM),
        scratch_shapes=[
            pltpu.VMEM((rows, width), jnp.float32),
            pltpu.VMEM((groups, rows, width), jnp.float32),
            pltpu.SemaphoreType.DMA((groups,)),
            pltpu.SemaphoreType.DMA((groups,)),
        ],
        compiler_params=pltpu.CompilerParams(collective_id=1, has_side_effects=True),
    )(layer_input, gate_weight)


def fold_t(left, right):
    return lax.dot_general(
        left, right, (((1,), (1,)), ((), ())), precision=highest,
        preferred_element_type=jnp.float32,
    )


def inverse_unit_lower(coupling, eye):
    length = coupling.shape[0]
    power = -coupling
    inverse = eye + power
    span = 2
    while span < length:
        power = fold(power, power)
        inverse = inverse + fold(inverse, power)
        span *= 2
    return inverse


def chunk_kernel(
    ext_ref, seg_ref, taps_ref, gates_ref,
    local_ref, reach_ref, carry_ref, inject_ref,
):
    length = local_ref.shape[1]
    heads = local_ref.shape[0]
    dk = carry_ref.shape[1]
    dv = local_ref.shape[2]
    edge = ext_ref.shape[0] - length
    q_end = heads * dk
    k_end = 2 * heads * dk

    own_seg = seg_ref[pl.ds(edge, length), :]
    summed = None
    for offset in range(edge + 1):
        term = jnp.where(
            seg_ref[pl.ds(offset, length), :] == own_seg,
            ext_ref[pl.ds(offset, length), :],
            0.0,
        ) * taps_ref[pl.ds(offset, 1), :]
        summed = term if summed is None else summed + term
    mixed_in = summed / (1.0 + jnp.exp(-summed))

    rows = lax.broadcasted_iota(jnp.int32, (length, length), 0)
    cols = lax.broadcasted_iota(jnp.int32, (length, length), 1)
    eye = (rows == cols).astype(jnp.float32)
    lower_ones = (rows >= cols).astype(jnp.float32)
    seg_grid = jnp.broadcast_to(own_seg, (length, length))
    same = seg_grid == jnp.transpose(seg_grid)
    causal = (rows >= cols) & same
    strict = (rows > cols) & same
    linked = (own_seg == seg_ref[pl.ds(edge - 1, 1), :]).astype(jnp.float32)
    tail = (own_seg == seg_ref[pl.ds(edge + length - 1, 1), :]).astype(jnp.float32)
    linked_last = linked[length - 1 :, :]

    for h in range(heads):
        queries = mixed_in[:, h * dk : (h + 1) * dk]
        key_raw = mixed_in[:, q_end + h * dk : q_end + (h + 1) * dk]
        values = mixed_in[:, k_end + h * dv : k_end + (h + 1) * dv]
        keys = key_raw * lax.rsqrt(jnp.sum(key_raw * key_raw, axis=1, keepdims=True) + 1e-06)
        log_alpha = gates_ref[:, h : h + 1]
        beta = gates_ref[:, heads + h : heads + h + 1]
        cum_grid = fold(lower_ones, jnp.broadcast_to(log_alpha, (length, length)))
        cumulative = cum_grid[:, 0:1]
        last = cum_grid[length - 1 :, 0:1]
        gap = cum_grid - jnp.transpose(cum_grid)
        decays = jnp.where(causal, jnp.exp(jnp.where(causal, gap, 0.0)), 0.0)
        coupling = beta * fold_t(keys, keys) * jnp.where(strict, decays, 0.0)
        inverse = inverse_unit_lower(coupling, eye)
        start_scale = jnp.exp(cumulative) * linked
        fresh = fold(inverse, beta * values)
        carried = fold(inverse, (beta * start_scale) * keys)
        scores = fold_t(queries, keys) * decays
        reach_ref[h] = queries * start_scale - fold(scores, carried)
        local_ref[h] = fold(scores, fresh)
        fade_out = jnp.exp(last - cumulative) * tail
        pushed_t = jnp.transpose(fade_out * keys)
        keep = linked_last * jnp.exp(last)
        carry_ref[h] = keep * eye - fold(pushed_t, carried)
        inject_ref[h] = fold(pushed_t, fresh)


def chunk_terms(ext, seg_ext, taps, gates, heads):
    length = ext.shape[0] - (CONV - 1)
    shapes = (
        jax.ShapeDtypeStruct((heads, length, DV), jnp.float32),
        jax.ShapeDtypeStruct((heads, length, DK), jnp.float32),
        jax.ShapeDtypeStruct((heads, DK, DK), jnp.float32),
        jax.ShapeDtypeStruct((heads, DK, DV), jnp.float32),
    )
    return pl.pallas_call(
        chunk_kernel,
        out_shape=shapes,
        in_specs=[pl.BlockSpec(memory_space=pltpu.VMEM)] * 4,
        out_specs=[pl.BlockSpec(memory_space=pltpu.VMEM)] * 4,
    )(ext, seg_ext, taps, gates)


def local(
    layer_input,
    q_in,
    k_in,
    v_in,
    z_in,
    conv_q,
    conv_k,
    conv_v,
    gate_weight,
    decay_rate,
    dt_bias,
    norm_gain,
    segment_ids,
):
    row_count = q_in.shape[0]
    local_heads = q_in.shape[1] // DK
    edge_rows = CONV - 1
    seg_marks = (segment_ids[row_count - edge_rows :] + 1).astype(jnp.bfloat16)[:, None]
    q_width, k_width = q_in.shape[1], k_in.shape[1]
    edges = jnp.concatenate(
        [
            q_in[row_count - edge_rows :],
            k_in[row_count - edge_rows :],
            v_in[row_count - edge_rows :],
            seg_marks,
        ],
        axis=1,
    )
    prior = passed_along(edges, "req", 1)
    prior_seg = prior[:, -1:].astype(jnp.float32) - 1.0
    ext = jnp.concatenate(
        [prior[:, :-1], jnp.concatenate([q_in, k_in, v_in], axis=1)], axis=0
    ).astype(jnp.float32)
    seg_ext = jnp.concatenate([prior_seg, segment_ids.astype(jnp.float32)[:, None]], axis=0)
    taps = jnp.concatenate([conv_q, conv_k, conv_v], axis=1).astype(jnp.float32)
    gate_total = gate_sum(layer_input, gate_weight, lax.axis_size("tp"))
    head_start = lax.axis_index("tp") * local_heads
    decay_in = lax.dynamic_slice_in_dim(gate_total, head_start, local_heads, 1)
    beta_in = lax.dynamic_slice_in_dim(gate_total, HEADS + head_start, local_heads, 1)
    log_alpha = -decay_rate[None, :] * jax.nn.softplus(decay_in + dt_bias[None, :])
    beta_gate = jax.nn.sigmoid(beta_in)
    gates = jnp.concatenate([log_alpha, beta_gate], axis=1)
    local_out, reach_back, carry_map, injected = chunk_terms(
        ext, seg_ext, taps, gates, local_heads
    )
    incoming = carried_in(carry_map, injected, lax.axis_size("req"))
    head_out = local_out + product("hcd,hde->hce", reach_back, incoming)
    head_out = jnp.transpose(head_out, (1, 0, 2))
    return finish(head_out, z_in, norm_gain)


def solution(mesh):
    placed = (
        P("req", "tp"),
        P("req", "tp"),
        P("req", "tp"),
        P("req", "tp"),
        P("req", "tp"),
        P(None, "tp"),
        P(None, "tp"),
        P(None, "tp"),
        P("tp", None),
        P("tp"),
        P("tp"),
        P(),
        P("req"),
    )
    return jax.shard_map(
        local, mesh=mesh, in_specs=placed, out_specs=P("req", "tp"), check_vma=False
    )
```

```python
import functools

import jax
import jax.numpy as jnp
from jax import lax
from jax.experimental import pallas as pl
from jax.experimental.pallas import tpu as pltpu
from jax.sharding import PartitionSpec as P

HEADS = 8
DK = 128
DV = 256
CONV = 4
EDGE = 16

MESH = pl.DeviceIdType.MESH
highest = lax.Precision.HIGHEST


def fold(high, low):
    return jnp.dot(high, low, precision=highest, preferred_element_type=jnp.float32)


def fold_t(left, right):
    return lax.dot_general(
        left, right, (((1,), (1,)), ((), ())), precision=highest,
        preferred_element_type=jnp.float32,
    )


def inverse_unit_lower(coupling, eye):
    length = coupling.shape[0]
    power = -coupling
    inverse = eye + power
    span = 2
    while span < length:
        power = fold(power, power)
        inverse = inverse + fold(inverse, power)
        span *= 2
    return inverse


def layer_kernel(
    devices, groups,
    x_ref, w_ref, q_ref, k_ref, v_ref, z_ref, cq_ref, ck_ref, cv_ref,
    decay_ref, bias_ref, gain_ref, seg_ref,
    out_ref,
    partial, got_gate, prev_q, prev_k, prev_v, prev_seg,
    local_sc, reach_sc, carry_sc, inject_sc, incoming,
    got1_a, got1_b, got2_a, got2_b, got3_b, got4_b,
    lo_a, lo_b, join_a, join_b, pair_a, pair_b, quad_b, reply,
    wire_a, wire_b, wire_pair, wire_quad,
    gate_send, gate_recv, edge_send, edge_recv, send_sems, recv_sems,
):
    me = lax.axis_index("req")
    tp_me = lax.axis_index("tp")
    core = lax.rem(me, 2)
    partner = me + 1 - 2 * core
    length = q_ref.shape[0]
    heads = carry_sc.shape[0]

    def at(device):
        return (lax.rem(device + devices, devices), tp_me)

    def across(step):
        return (me, lax.rem(tp_me + step, groups))

    barrier = pltpu.get_barrier_semaphore()
    for shift in (1, 2, 4):
        for peer in (me + shift, me - shift):
            pl.semaphore_signal(barrier, inc=1, device_id=at(peer), device_id_type=MESH)
    for step in range(1, groups):
        pl.semaphore_signal(barrier, inc=1, device_id=across(step), device_id_type=MESH)
    pl.semaphore_wait(barrier, 6 + groups - 1)

    edge_pairs = (
        (q_ref.at[pl.ds(length - EDGE, EDGE), :], prev_q.at[pl.ds(length - EDGE, EDGE), :]),
        (k_ref.at[pl.ds(length - EDGE, EDGE), :], prev_k.at[pl.ds(length - EDGE, EDGE), :]),
        (v_ref.at[pl.ds(length - EDGE, EDGE), :], prev_v.at[pl.ds(length - EDGE, EDGE), :]),
        (seg_ref, prev_seg),
    )
    edge_copies = [
        pltpu.make_async_remote_copy(
            src_ref=src, dst_ref=dst, send_sem=edge_send.at[slot], recv_sem=edge_recv.at[slot],
            device_id=at(me + 1), device_id_type=MESH,
        )
        for slot, (src, dst) in enumerate(edge_pairs)
    ]

    @pl.when(me + 1 < devices)
    def _():
        for copy in edge_copies:
            copy.start()

    partial[...] = jnp.dot(x_ref[...], w_ref[...], preferred_element_type=jnp.float32)
    gate_copies = [
        pltpu.make_async_remote_copy(
            src_ref=partial, dst_ref=got_gate.at[tp_me], send_sem=gate_send.at[step],
            recv_sem=gate_recv.at[tp_me], device_id=across(step), device_id_type=MESH,
        )
        for step in range(1, groups)
    ]
    for copy in gate_copies:
        copy.start()

    for buffer in (prev_q, prev_k, prev_v):
        buffer[pl.ds(0, length - EDGE), :] = jnp.zeros(
            (length - EDGE, buffer.shape[1]), buffer.dtype
        )

    @pl.when(me >= 1)
    def _():
        for copy in edge_copies:
            copy.wait_recv()

    @pl.when(me < 1)
    def _():
        for buffer in (prev_q, prev_k, prev_v):
            buffer[pl.ds(length - EDGE, EDGE), :] = jnp.zeros(
                (EDGE, buffer.shape[1]), buffer.dtype
            )
        prev_seg[...] = jnp.full(prev_seg.shape, -1, prev_seg.dtype)

    rows = lax.broadcasted_iota(jnp.int32, (length, length), 0)
    cols = lax.broadcasted_iota(jnp.int32, (length, length), 1)
    eye = (rows == cols).astype(jnp.float32)
    lower_ones = (rows >= cols).astype(jnp.float32)
    seg_cols = jnp.transpose(jnp.broadcast_to(seg_ref[...].astype(jnp.float32), (length, length)))
    prev_cols = jnp.transpose(
        jnp.broadcast_to(prev_seg[...].astype(jnp.float32), (length, length))
    )
    own_seg = seg_cols[:, 0:1]
    token = rows[:, 0:1]

    def shifted(own, prev, shift):
        return jnp.where(token >= shift, pltpu.roll(own, shift, 0), pltpu.roll(prev, shift, 0))

    seg_before = [None] + [shifted(seg_cols, prev_cols, s)[:, 0:1] for s in range(1, CONV)]

    def short_conv(own_ref, prev_ref, taps_ref):
        own = own_ref[...].astype(jnp.float32)
        prev = prev_ref[...].astype(jnp.float32)
        summed = None
        for offset in range(CONV):
            shift = CONV - 1 - offset
            if shift == 0:
                term = own
            else:
                term = jnp.where(
                    seg_before[shift] == own_seg, shifted(own, prev, shift), 0.0
                )
            term = term * taps_ref[pl.ds(offset, 1), :].astype(jnp.float32)
            summed = term if summed is None else summed + term
        return summed / (1.0 + jnp.exp(-summed))

    queries_all = short_conv(q_ref, prev_q, cq_ref)
    keys_all = short_conv(k_ref, prev_k, ck_ref)
    values_all = short_conv(v_ref, prev_v, cv_ref)

    for step in range(1, groups):
        source = lax.rem(tp_me + step, groups)
        pltpu.make_async_remote_copy(
            src_ref=partial, dst_ref=got_gate.at[source], send_sem=gate_send.at[0],
            recv_sem=gate_recv.at[source], device_id=(me, source), device_id_type=MESH,
        ).wait_recv()
    gate_total = None
    for source in range(groups):
        term = jnp.where(source == tp_me, partial[...], got_gate[source])
        gate_total = term if gate_total is None else gate_total + term
    lanes = lax.broadcasted_iota(jnp.int32, gate_total.shape, 1)

    seg_grid = jnp.broadcast_to(own_seg, (length, length))
    same = seg_grid == jnp.transpose(seg_grid)
    causal = (rows >= cols) & same
    strict = (rows > cols) & same
    linked = (own_seg == prev_cols[length - 1 :, 0:1]).astype(jnp.float32)
    tail = (own_seg == own_seg[length - 1 :, :]).astype(jnp.float32)
    linked_last = linked[length - 1 :, :]

    for h in range(heads):
        column = tp_me * heads + h
        decay_in = jnp.sum(jnp.where(lanes == column, gate_total, 0.0), axis=1, keepdims=True)
        beta_in = jnp.sum(
            jnp.where(lanes == HEADS + column, gate_total, 0.0), axis=1, keepdims=True
        )
        shifted_in = decay_in + bias_ref[h]
        softplus = jnp.maximum(shifted_in, 0.0) + jnp.log1p(jnp.exp(-jnp.abs(shifted_in)))
        log_alpha = -decay_ref[h] * softplus
        beta = 1.0 / (1.0 + jnp.exp(-beta_in))

        queries = queries_all[:, h * DK : (h + 1) * DK]
        key_raw = keys_all[:, h * DK : (h + 1) * DK]
        values = values_all[:, h * DV : (h + 1) * DV]
        keys = key_raw * lax.rsqrt(jnp.sum(key_raw * key_raw, axis=1, keepdims=True) + 1e-06)
        cum_grid = fold(lower_ones, jnp.broadcast_to(log_alpha, (length, length)))
        cumulative = cum_grid[:, 0:1]
        last = cum_grid[length - 1 :, 0:1]
        gap = cum_grid - jnp.transpose(cum_grid)
        decays = jnp.where(causal, jnp.exp(jnp.where(causal, gap, 0.0)), 0.0)
        coupling = beta * fold_t(keys, keys) * jnp.where(strict, decays, 0.0)
        inverse = inverse_unit_lower(coupling, eye)
        start_scale = jnp.exp(cumulative) * linked
        fresh = fold(inverse, beta * values)
        carried = fold(inverse, (beta * start_scale) * keys)
        fade_out = jnp.exp(last - cumulative) * tail
        pushed_t = jnp.transpose(fade_out * keys)
        keep = linked_last * jnp.exp(last)
        carry_sc[h] = keep * eye - fold(pushed_t, carried)
        inject_sc[h] = fold(pushed_t, fresh)
        scores = fold_t(queries, keys) * decays
        reach_sc[h] = queries * start_scale - fold(scores, carried)
        local_sc[h] = fold(scores, fresh)

    for copy in gate_copies:
        copy.wait_send()

    @pl.when(me + 1 < devices)
    def _():
        for copy in edge_copies:
            copy.wait_send()

    def remote(step, slot, src, dst, target):
        return pltpu.make_async_remote_copy(
            src_ref=src, dst_ref=dst,
            send_sem=send_sems.at[step, slot], recv_sem=recv_sems.at[step, slot],
            device_id=at(target), device_id_type=MESH,
        )

    def along(step, pairs, shift):
        copies = [remote(step, slot, src, dst, me + shift) for slot, (src, dst) in enumerate(pairs)]

        @pl.when(me + shift < devices)
        def _():
            for copy in copies:
                copy.start()

        @pl.when(me >= shift)
        def _():
            for copy in copies:
                copy.wait_recv()

        @pl.when(me < shift)
        def _():
            for _, dst in pairs:
                dst[...] = jnp.zeros(dst.shape, dst.dtype)

        return copies

    def sent(copies, shift):
        @pl.when(me + shift < devices)
        def _():
            for copy in copies:
                copy.wait_send()

    first = [
        remote(0, 0, carry_sc.at[1 - core], got1_a, partner),
        remote(0, 1, inject_sc.at[1 - core], got1_b, partner),
    ]
    for copy in first:
        copy.start()
    for copy in first:
        copy.wait_recv()
    own_a = carry_sc[core]
    own_b = inject_sc[core]
    low = core == 0
    lo_a[...] = jnp.where(low, own_a, got1_a[...])
    lo_b[...] = jnp.where(low, own_b, got1_b[...])
    hi_a = jnp.where(low, got1_a[...], own_a)
    hi_b = jnp.where(low, got1_b[...], own_b)
    join_a[...] = fold(hi_a, lo_a[...])
    join_b[...] = fold(hi_a, lo_b[...]) + hi_b
    wire_a[...] = join_a[...].astype(wire_a.dtype)
    wire_b[...] = join_b[...].astype(wire_b.dtype)
    for copy in first:
        copy.wait_send()

    copies = along(1, ((wire_a, got2_a), (wire_b, got2_b)), 2)
    pair_a[...] = fold(join_a[...], got2_a[...].astype(jnp.float32))
    pair_b[...] = fold(join_a[...], got2_b[...].astype(jnp.float32)) + join_b[...]
    wire_pair[...] = pair_b[...].astype(wire_pair.dtype)
    sent(copies, 2)

    copies = along(2, ((wire_pair, got3_b),), 4)
    quad_b[...] = fold(pair_a[...], got3_b[...].astype(jnp.float32)) + pair_b[...]
    wire_quad[...] = quad_b[...].astype(wire_quad.dtype)
    sent(copies, 4)

    copies = along(3, ((wire_quad, got4_b),), 2)
    entering = got4_b[...].astype(jnp.float32)
    onward = fold(lo_a[...], entering) + lo_b[...]
    sent(copies, 2)

    reply[...] = jnp.where(low, onward, entering)
    last_copy = remote(4, 0, reply, incoming.at[core], partner)
    last_copy.start()
    incoming[core] = jnp.where(low, entering, onward)
    remote(4, 0, reply, incoming.at[1 - core], partner).wait_recv()

    gain = gain_ref[...].astype(jnp.float32)
    for h in range(heads):
        head_out = local_sc[h] + fold(reach_sc[h], incoming[h])
        scale = lax.rsqrt(jnp.mean(head_out * head_out, axis=1, keepdims=True) + 1e-06)
        z_part = z_ref[:, h * DV : (h + 1) * DV].astype(jnp.float32)
        gating = z_part / (1.0 + jnp.exp(-z_part))
        out_ref[:, h * DV : (h + 1) * DV] = (head_out * scale * gain * gating).astype(
            out_ref.dtype
        )
    last_copy.wait_send()


def local(
    layer_input, q_in, k_in, v_in, z_in, conv_q, conv_k, conv_v,
    gate_weight, decay_rate, dt_bias, norm_gain, segment_ids,
):
    length = q_in.shape[0]
    heads = q_in.shape[1] // DK
    devices = lax.axis_size("req")
    groups = lax.axis_size("tp")
    f32 = jnp.float32
    a_shape = pltpu.VMEM((DK, DK), f32)
    b_shape = pltpu.VMEM((DK, DV), f32)
    a_wire = pltpu.VMEM((DK, DK), jnp.bfloat16)
    b_wire = pltpu.VMEM((DK, DV), jnp.bfloat16)
    vmem = pl.BlockSpec(memory_space=pltpu.VMEM)
    smem = pl.BlockSpec(memory_space=pltpu.SMEM)
    return pl.pallas_call(
        functools.partial(layer_kernel, devices, groups),
        out_shape=jax.ShapeDtypeStruct(z_in.shape, jnp.bfloat16),
        in_specs=[vmem] * 9 + [smem, smem, vmem, vmem],
        out_specs=vmem,
        scratch_shapes=[
            pltpu.VMEM((length, gate_weight.shape[1]), f32),
            pltpu.VMEM((groups, length, gate_weight.shape[1]), f32),
            pltpu.VMEM(q_in.shape, q_in.dtype),
            pltpu.VMEM(k_in.shape, k_in.dtype),
            pltpu.VMEM(v_in.shape, v_in.dtype),
            pltpu.VMEM((1, length), segment_ids.dtype),
            pltpu.VMEM((heads, length, DV), f32),
            pltpu.VMEM((heads, length, DK), f32),
            pltpu.VMEM((heads, DK, DK), f32),
            pltpu.VMEM((heads, DK, DV), f32),
            pltpu.VMEM((heads, DK, DV), f32),
            a_shape, b_shape, a_wire, b_wire, b_wire, b_wire,
            a_shape, b_shape, a_shape, b_shape, a_shape, b_shape, b_shape, b_shape,
            a_wire, b_wire, b_wire, b_wire,
            pltpu.SemaphoreType.DMA((groups,)),
            pltpu.SemaphoreType.DMA((groups,)),
            pltpu.SemaphoreType.DMA((4,)),
            pltpu.SemaphoreType.DMA((4,)),
            pltpu.SemaphoreType.DMA((5, 2)),
            pltpu.SemaphoreType.DMA((5, 2)),
        ],
        compiler_params=pltpu.CompilerParams(collective_id=0, has_side_effects=True),
    )(
        layer_input, gate_weight, q_in, k_in, v_in, z_in, conv_q, conv_k, conv_v,
        decay_rate, dt_bias, norm_gain.reshape(1, -1), segment_ids.reshape(1, -1),
    )


def solution(mesh):
    placed = (
        P("req", "tp"),
        P("req", "tp"),
        P("req", "tp"),
        P("req", "tp"),
        P("req", "tp"),
        P(None, "tp"),
        P(None, "tp"),
        P(None, "tp"),
        P("tp", None),
        P("tp"),
        P("tp"),
        P(),
        P("req"),
    )
    return jax.shard_map(
        local, mesh=mesh, in_specs=placed, out_specs=P("req", "tp"), check_vma=False
    )
```

```python
import functools

import jax
import jax.numpy as jnp
from jax import lax
from jax.experimental import pallas as pl
from jax.experimental.pallas import tpu as pltpu
from jax.sharding import PartitionSpec as P

HEADS = 8
DK = 128
DV = 256
CONV = 4
EDGE = 16

MESH = pl.DeviceIdType.MESH
highest = lax.Precision.HIGHEST


def fold(high, low):
    return jnp.dot(high, low, precision=highest, preferred_element_type=jnp.float32)


def fold_t(left, right):
    return lax.dot_general(
        left, right, (((1,), (1,)), ((), ())), precision=highest,
        preferred_element_type=jnp.float32,
    )


def inverse_unit_lower(coupling, eye):
    length = coupling.shape[0]
    power = -coupling
    inverse = eye + power
    span = 2
    while span < length:
        power = fold(power, power)
        inverse = inverse + fold(inverse, power)
        span *= 2
    return inverse


def layer_kernel(
    devices, groups,
    x_ref, w_ref, q_ref, k_ref, v_ref, z_ref, cq_ref, ck_ref, cv_ref,
    decay_ref, bias_ref, gain_ref, seg_ref,
    out_ref,
    partial, got_gate, prev_q, prev_k, prev_v, prev_seg,
    local_sc, reach_sc, carry_sc, inject_sc, incoming,
    keys_sc, decay_sc, start_sc, fresh_sc, carried_sc,
    got1_a, got1_b, got2_a, got2_b, got3_b, got4_b,
    lo_a, lo_b, join_a, join_b, pair_a, pair_b, quad_b, reply,
    wire_a, wire_b, wire_pair, wire_quad,
    gate_send, gate_recv, edge_send, edge_recv, send_sems, recv_sems,
):
    me = lax.axis_index("req")
    tp_me = lax.axis_index("tp")
    core = lax.rem(me, 2)
    partner = me + 1 - 2 * core
    length = q_ref.shape[0]
    heads = carry_sc.shape[0]

    def at(device):
        return (lax.rem(device + devices, devices), tp_me)

    def across(step):
        return (me, lax.rem(tp_me + step, groups))

    barrier = pltpu.get_barrier_semaphore()
    for shift in (1, 2, 4):
        for peer in (me + shift, me - shift):
            pl.semaphore_signal(barrier, inc=1, device_id=at(peer), device_id_type=MESH)
    for step in range(1, groups):
        pl.semaphore_signal(barrier, inc=1, device_id=across(step), device_id_type=MESH)
    pl.semaphore_wait(barrier, 6 + groups - 1)

    edge_pairs = (
        (q_ref.at[pl.ds(length - EDGE, EDGE), :], prev_q.at[pl.ds(length - EDGE, EDGE), :]),
        (k_ref.at[pl.ds(length - EDGE, EDGE), :], prev_k.at[pl.ds(length - EDGE, EDGE), :]),
        (v_ref.at[pl.ds(length - EDGE, EDGE), :], prev_v.at[pl.ds(length - EDGE, EDGE), :]),
        (seg_ref, prev_seg),
    )
    edge_copies = [
        pltpu.make_async_remote_copy(
            src_ref=src, dst_ref=dst, send_sem=edge_send.at[slot], recv_sem=edge_recv.at[slot],
            device_id=at(me + 1), device_id_type=MESH,
        )
        for slot, (src, dst) in enumerate(edge_pairs)
    ]

    @pl.when(me + 1 < devices)
    def _():
        for copy in edge_copies:
            copy.start()

    partial[...] = jnp.dot(x_ref[...], w_ref[...], preferred_element_type=jnp.float32)
    gate_copies = [
        pltpu.make_async_remote_copy(
            src_ref=partial, dst_ref=got_gate.at[tp_me], send_sem=gate_send.at[step],
            recv_sem=gate_recv.at[tp_me], device_id=across(step), device_id_type=MESH,
        )
        for step in range(1, groups)
    ]
    for copy in gate_copies:
        copy.start()

    for buffer in (prev_q, prev_k, prev_v):
        buffer[pl.ds(0, length - EDGE), :] = jnp.zeros(
            (length - EDGE, buffer.shape[1]), buffer.dtype
        )

    @pl.when(me >= 1)
    def _():
        for copy in edge_copies:
            copy.wait_recv()

    @pl.when(me < 1)
    def _():
        for buffer in (prev_q, prev_k, prev_v):
            buffer[pl.ds(length - EDGE, EDGE), :] = jnp.zeros(
                (EDGE, buffer.shape[1]), buffer.dtype
            )
        prev_seg[...] = jnp.full(prev_seg.shape, -1, prev_seg.dtype)

    rows = lax.broadcasted_iota(jnp.int32, (length, length), 0)
    cols = lax.broadcasted_iota(jnp.int32, (length, length), 1)
    eye = (rows == cols).astype(jnp.float32)
    lower_ones = (rows >= cols).astype(jnp.float32)
    seg_cols = jnp.transpose(jnp.broadcast_to(seg_ref[...].astype(jnp.float32), (length, length)))
    prev_cols = jnp.transpose(
        jnp.broadcast_to(prev_seg[...].astype(jnp.float32), (length, length))
    )
    own_seg = seg_cols[:, 0:1]
    token = rows[:, 0:1]

    def shifted(own, prev, shift):
        return jnp.where(token >= shift, pltpu.roll(own, shift, 0), pltpu.roll(prev, shift, 0))

    seg_before = [None] + [shifted(seg_cols, prev_cols, s)[:, 0:1] for s in range(1, CONV)]

    def short_conv(own_ref, prev_ref, taps_ref):
        own = own_ref[...].astype(jnp.float32)
        prev = prev_ref[...].astype(jnp.float32)
        summed = None
        for offset in range(CONV):
            shift = CONV - 1 - offset
            if shift == 0:
                term = own
            else:
                term = jnp.where(
                    seg_before[shift] == own_seg, shifted(own, prev, shift), 0.0
                )
            term = term * taps_ref[pl.ds(offset, 1), :].astype(jnp.float32)
            summed = term if summed is None else summed + term
        return summed / (1.0 + jnp.exp(-summed))

    queries_all = short_conv(q_ref, prev_q, cq_ref)
    keys_all = short_conv(k_ref, prev_k, ck_ref)
    values_all = short_conv(v_ref, prev_v, cv_ref)

    for step in range(1, groups):
        source = lax.rem(tp_me + step, groups)
        pltpu.make_async_remote_copy(
            src_ref=partial, dst_ref=got_gate.at[source], send_sem=gate_send.at[0],
            recv_sem=gate_recv.at[source], device_id=(me, source), device_id_type=MESH,
        ).wait_recv()
    gate_total = None
    for source in range(groups):
        term = jnp.where(source == tp_me, partial[...], got_gate[source])
        gate_total = term if gate_total is None else gate_total + term
    lanes = lax.broadcasted_iota(jnp.int32, gate_total.shape, 1)

    seg_grid = jnp.broadcast_to(own_seg, (length, length))
    same = seg_grid == jnp.transpose(seg_grid)
    causal = (rows >= cols) & same
    strict = (rows > cols) & same
    linked = (own_seg == prev_cols[length - 1 :, 0:1]).astype(jnp.float32)
    tail = (own_seg == own_seg[length - 1 :, :]).astype(jnp.float32)
    linked_last = linked[length - 1 :, :]

    def head_terms(h):
        column = tp_me * heads + h
        decay_in = jnp.sum(jnp.where(lanes == column, gate_total, 0.0), axis=1, keepdims=True)
        beta_in = jnp.sum(
            jnp.where(lanes == HEADS + column, gate_total, 0.0), axis=1, keepdims=True
        )
        shifted_in = decay_in + bias_ref[h]
        softplus = jnp.maximum(shifted_in, 0.0) + jnp.log1p(jnp.exp(-jnp.abs(shifted_in)))
        log_alpha = -decay_ref[h] * softplus
        beta = 1.0 / (1.0 + jnp.exp(-beta_in))

        key_raw = keys_all[:, h * DK : (h + 1) * DK]
        values = values_all[:, h * DV : (h + 1) * DV]
        keys = key_raw * lax.rsqrt(jnp.sum(key_raw * key_raw, axis=1, keepdims=True) + 1e-06)
        cum_grid = fold(lower_ones, jnp.broadcast_to(log_alpha, (length, length)))
        cumulative = cum_grid[:, 0:1]
        last = cum_grid[length - 1 :, 0:1]
        gap = cum_grid - jnp.transpose(cum_grid)
        decays = jnp.where(causal, jnp.exp(jnp.where(causal, gap, 0.0)), 0.0)
        coupling = beta * fold_t(keys, keys) * jnp.where(strict, decays, 0.0)
        inverse = inverse_unit_lower(coupling, eye)
        start_scale = jnp.exp(cumulative) * linked
        fresh = fold(inverse, beta * values)
        carried = fold(inverse, (beta * start_scale) * keys)
        fade_out = jnp.exp(last - cumulative) * tail
        pushed_t = jnp.transpose(fade_out * keys)
        keep = linked_last * jnp.exp(last)
        carry_sc[h] = keep * eye - fold(pushed_t, carried)
        inject_sc[h] = fold(pushed_t, fresh)
        keys_sc[h] = keys
        decay_sc[h] = decays
        start_sc[h] = jnp.broadcast_to(start_scale, (length, DK))
        fresh_sc[h] = fresh
        carried_sc[h] = carried

    def head_outputs(h):
        queries = queries_all[:, h * DK : (h + 1) * DK]
        scores = fold_t(queries, keys_sc[h]) * decay_sc[h]
        reach_sc[h] = queries * start_sc[h] - fold(scores, carried_sc[h])
        local_sc[h] = fold(scores, fresh_sc[h])

    def remote(step, slot, src, dst, target):
        return pltpu.make_async_remote_copy(
            src_ref=src, dst_ref=dst,
            send_sem=send_sems.at[step, slot], recv_sem=recv_sems.at[step, slot],
            device_id=at(target), device_id_type=MESH,
        )

    def launch(step, pairs, shift):
        copies = [remote(step, slot, src, dst, me + shift) for slot, (src, dst) in enumerate(pairs)]

        @pl.when(me + shift < devices)
        def _():
            for copy in copies:
                copy.start()

        return copies

    def land(copies, pairs, shift):
        @pl.when(me >= shift)
        def _():
            for copy in copies:
                copy.wait_recv()

        @pl.when(me < shift)
        def _():
            for _, dst in pairs:
                dst[...] = jnp.zeros(dst.shape, dst.dtype)

        return copies

    def sent(copies, shift):
        @pl.when(me + shift < devices)
        def _():
            for copy in copies:
                copy.wait_send()

    first = [
        remote(0, 0, carry_sc.at[1 - core], got1_a, partner),
        remote(0, 1, inject_sc.at[1 - core], got1_b, partner),
    ]
    for own_head in range(heads):

        @pl.when(core == own_head)
        def _():
            head_terms(1 - own_head)
            for copy in first:
                copy.start()
            head_terms(own_head)

    for copy in gate_copies:
        copy.wait_send()

    @pl.when(me + 1 < devices)
    def _():
        for copy in edge_copies:
            copy.wait_send()

    for copy in first:
        copy.wait_recv()
    own_a = carry_sc[core]
    own_b = inject_sc[core]
    low = core == 0
    lo_a[...] = jnp.where(low, own_a, got1_a[...])
    lo_b[...] = jnp.where(low, own_b, got1_b[...])
    hi_a = jnp.where(low, got1_a[...], own_a)
    hi_b = jnp.where(low, got1_b[...], own_b)
    join_a[...] = fold(hi_a, lo_a[...])
    join_b[...] = fold(hi_a, lo_b[...]) + hi_b
    wire_a[...] = join_a[...].astype(wire_a.dtype)
    wire_b[...] = join_b[...].astype(wire_b.dtype)
    for copy in first:
        copy.wait_send()

    pairs = ((wire_a, got2_a), (wire_b, got2_b))
    copies = launch(1, pairs, 2)
    head_outputs(0)
    land(copies, pairs, 2)
    pair_a[...] = fold(join_a[...], got2_a[...].astype(jnp.float32))
    pair_b[...] = fold(join_a[...], got2_b[...].astype(jnp.float32)) + join_b[...]
    wire_pair[...] = pair_b[...].astype(wire_pair.dtype)
    sent(copies, 2)

    pairs = ((wire_pair, got3_b),)
    copies = launch(2, pairs, 4)
    head_outputs(1)
    land(copies, pairs, 4)
    quad_b[...] = fold(pair_a[...], got3_b[...].astype(jnp.float32)) + pair_b[...]
    wire_quad[...] = quad_b[...].astype(wire_quad.dtype)
    sent(copies, 4)

    pairs = ((wire_quad, got4_b),)
    copies = launch(3, pairs, 2)
    land(copies, pairs, 2)
    entering = got4_b[...].astype(jnp.float32)
    onward = fold(lo_a[...], entering) + lo_b[...]
    sent(copies, 2)

    reply[...] = jnp.where(low, onward, entering)
    last_copy = remote(4, 0, reply, incoming.at[core], partner)
    last_copy.start()
    incoming[core] = jnp.where(low, entering, onward)
    remote(4, 0, reply, incoming.at[1 - core], partner).wait_recv()

    gain = gain_ref[...].astype(jnp.float32)
    for h in range(heads):
        head_out = local_sc[h] + fold(reach_sc[h], incoming[h])
        scale = lax.rsqrt(jnp.mean(head_out * head_out, axis=1, keepdims=True) + 1e-06)
        z_part = z_ref[:, h * DV : (h + 1) * DV].astype(jnp.float32)
        gating = z_part / (1.0 + jnp.exp(-z_part))
        out_ref[:, h * DV : (h + 1) * DV] = (head_out * scale * gain * gating).astype(
            out_ref.dtype
        )
    last_copy.wait_send()


def local(
    layer_input, q_in, k_in, v_in, z_in, conv_q, conv_k, conv_v,
    gate_weight, decay_rate, dt_bias, norm_gain, segment_ids,
):
    length = q_in.shape[0]
    heads = q_in.shape[1] // DK
    devices = lax.axis_size("req")
    groups = lax.axis_size("tp")
    f32 = jnp.float32
    a_shape = pltpu.VMEM((DK, DK), f32)
    b_shape = pltpu.VMEM((DK, DV), f32)
    a_wire = pltpu.VMEM((DK, DK), jnp.bfloat16)
    b_wire = pltpu.VMEM((DK, DV), jnp.bfloat16)
    vmem = pl.BlockSpec(memory_space=pltpu.VMEM)
    smem = pl.BlockSpec(memory_space=pltpu.SMEM)
    return pl.pallas_call(
        functools.partial(layer_kernel, devices, groups),
        out_shape=jax.ShapeDtypeStruct(z_in.shape, jnp.bfloat16),
        in_specs=[vmem] * 9 + [smem, smem, vmem, vmem],
        out_specs=vmem,
        scratch_shapes=[
            pltpu.VMEM((length, gate_weight.shape[1]), f32),
            pltpu.VMEM((groups, length, gate_weight.shape[1]), f32),
            pltpu.VMEM(q_in.shape, q_in.dtype),
            pltpu.VMEM(k_in.shape, k_in.dtype),
            pltpu.VMEM(v_in.shape, v_in.dtype),
            pltpu.VMEM((1, length), segment_ids.dtype),
            pltpu.VMEM((heads, length, DV), f32),
            pltpu.VMEM((heads, length, DK), f32),
            pltpu.VMEM((heads, DK, DK), f32),
            pltpu.VMEM((heads, DK, DV), f32),
            pltpu.VMEM((heads, DK, DV), f32),
            pltpu.VMEM((heads, length, DK), f32),
            pltpu.VMEM((heads, length, length), f32),
            pltpu.VMEM((heads, length, DK), f32),
            pltpu.VMEM((heads, length, DV), f32),
            pltpu.VMEM((heads, length, DK), f32),
            a_shape, b_shape, a_wire, b_wire, b_wire, b_wire,
            a_shape, b_shape, a_shape, b_shape, a_shape, b_shape, b_shape, b_shape,
            a_wire, b_wire, b_wire, b_wire,
            pltpu.SemaphoreType.DMA((groups,)),
            pltpu.SemaphoreType.DMA((groups,)),
            pltpu.SemaphoreType.DMA((4,)),
            pltpu.SemaphoreType.DMA((4,)),
            pltpu.SemaphoreType.DMA((5, 2)),
            pltpu.SemaphoreType.DMA((5, 2)),
        ],
        compiler_params=pltpu.CompilerParams(collective_id=0, has_side_effects=True),
    )(
        layer_input, gate_weight, q_in, k_in, v_in, z_in, conv_q, conv_k, conv_v,
        decay_rate, dt_bias, norm_gain.reshape(1, -1), segment_ids.reshape(1, -1),
    )


def solution(mesh):
    placed = (
        P("req", "tp"),
        P("req", "tp"),
        P("req", "tp"),
        P("req", "tp"),
        P("req", "tp"),
        P(None, "tp"),
        P(None, "tp"),
        P(None, "tp"),
        P("tp", None),
        P("tp"),
        P("tp"),
        P(),
        P("req"),
    )
    return jax.shard_map(
        local, mesh=mesh, in_specs=placed, out_specs=P("req", "tp"), check_vma=False
    )
```

```python
import functools

import jax
import jax.numpy as jnp
from jax import lax
from jax.experimental import pallas as pl
from jax.experimental.pallas import tpu as pltpu
from jax.sharding import PartitionSpec as P

HEADS = 8
DK = 128
DV = 256
CONV = 4
EDGE = 16

MESH = pl.DeviceIdType.MESH
highest = lax.Precision.HIGHEST


def fold(high, low):
    return jnp.dot(high, low, precision=highest, preferred_element_type=jnp.float32)


def fold_t(left, right):
    return lax.dot_general(
        left, right, (((1,), (1,)), ((), ())), precision=highest,
        preferred_element_type=jnp.float32,
    )


def inverse_unit_lower(coupling, eye):
    length = coupling.shape[0]
    power = -coupling
    inverse = eye + power
    span = 2
    while span < length:
        power = fold(power, power)
        inverse = inverse + fold(inverse, power)
        span *= 2
    return inverse


def layer_kernel(
    devices, groups,
    x_ref, w_ref, q_ref, k_ref, v_ref, z_ref, cq_ref, ck_ref, cv_ref,
    decay_ref, bias_ref, gain_ref, seg_ref,
    out_ref,
    partial, got_gate, prev_q, prev_k, prev_v, prev_seg,
    local_sc, reach_sc, carry_sc, inject_sc, incoming,
    keys_sc, decay_sc, start_sc, fresh_sc, carried_sc,
    got1_a, got1_b, got2_a, got2_b, got3_b, got4_b,
    lo_a, lo_b, join_a, join_b, pair_a, pair_b, quad_b, reply,
    wire_a, wire_b, wire_pair, wire_quad,
    gate_send, gate_recv, edge_send, edge_recv, send_sems, recv_sems,
):
    me = lax.axis_index("req")
    tp_me = lax.axis_index("tp")
    core = lax.rem(me, 2)
    partner = me + 1 - 2 * core
    length = q_ref.shape[0]
    heads = carry_sc.shape[0]

    def at(device):
        return (lax.rem(device + devices, devices), tp_me)

    def across(step):
        return (me, lax.rem(tp_me + step, groups))

    barrier = pltpu.get_barrier_semaphore()
    expected = groups - 1
    for shift in (1, 2, 4):

        @pl.when(me + shift < devices)
        def _():
            pl.semaphore_signal(barrier, inc=1, device_id=at(me + shift), device_id_type=MESH)

        @pl.when(me >= shift)
        def _():
            pl.semaphore_signal(barrier, inc=1, device_id=at(me - shift), device_id_type=MESH)

        expected = expected + (me + shift < devices).astype(jnp.int32)
        expected = expected + (me >= shift).astype(jnp.int32)
    for step in range(1, groups):
        pl.semaphore_signal(barrier, inc=1, device_id=across(step), device_id_type=MESH)
    pl.semaphore_wait(barrier, expected)

    edge_pairs = (
        (q_ref.at[pl.ds(length - EDGE, EDGE), :], prev_q.at[pl.ds(length - EDGE, EDGE), :]),
        (k_ref.at[pl.ds(length - EDGE, EDGE), :], prev_k.at[pl.ds(length - EDGE, EDGE), :]),
        (v_ref.at[pl.ds(length - EDGE, EDGE), :], prev_v.at[pl.ds(length - EDGE, EDGE), :]),
        (seg_ref, prev_seg),
    )
    edge_copies = [
        pltpu.make_async_remote_copy(
            src_ref=src, dst_ref=dst, send_sem=edge_send.at[slot], recv_sem=edge_recv.at[slot],
            device_id=at(me + 1), device_id_type=MESH,
        )
        for slot, (src, dst) in enumerate(edge_pairs)
    ]

    @pl.when(me + 1 < devices)
    def _():
        for copy in edge_copies:
            copy.start()

    partial[...] = jnp.dot(x_ref[...], w_ref[...], preferred_element_type=jnp.float32)
    gate_copies = [
        pltpu.make_async_remote_copy(
            src_ref=partial, dst_ref=got_gate.at[tp_me], send_sem=gate_send.at[step],
            recv_sem=gate_recv.at[tp_me], device_id=across(step), device_id_type=MESH,
        )
        for step in range(1, groups)
    ]
    for copy in gate_copies:
        copy.start()

    for buffer in (prev_q, prev_k, prev_v):
        buffer[pl.ds(0, length - EDGE), :] = jnp.zeros(
            (length - EDGE, buffer.shape[1]), buffer.dtype
        )

    @pl.when(me >= 1)
    def _():
        for copy in edge_copies:
            copy.wait_recv()

    @pl.when(me < 1)
    def _():
        for buffer in (prev_q, prev_k, prev_v):
            buffer[pl.ds(length - EDGE, EDGE), :] = jnp.zeros(
                (EDGE, buffer.shape[1]), buffer.dtype
            )
        prev_seg[...] = jnp.full(prev_seg.shape, -1, prev_seg.dtype)

    rows = lax.broadcasted_iota(jnp.int32, (length, length), 0)
    cols = lax.broadcasted_iota(jnp.int32, (length, length), 1)
    eye = (rows == cols).astype(jnp.float32)
    lower_ones = (rows >= cols).astype(jnp.float32)
    seg_cols = jnp.transpose(jnp.broadcast_to(seg_ref[...].astype(jnp.float32), (length, length)))
    prev_cols = jnp.transpose(
        jnp.broadcast_to(prev_seg[...].astype(jnp.float32), (length, length))
    )
    own_seg = seg_cols[:, 0:1]
    token = rows[:, 0:1]

    def shifted(own, prev, shift):
        return jnp.where(token >= shift, pltpu.roll(own, shift, 0), pltpu.roll(prev, shift, 0))

    seg_before = [None] + [shifted(seg_cols, prev_cols, s)[:, 0:1] for s in range(1, CONV)]

    def short_conv(own_ref, prev_ref, taps_ref):
        own = own_ref[...].astype(jnp.float32)
        prev = prev_ref[...].astype(jnp.float32)
        summed = None
        for offset in range(CONV):
            shift = CONV - 1 - offset
            if shift == 0:
                term = own
            else:
                term = jnp.where(
                    seg_before[shift] == own_seg, shifted(own, prev, shift), 0.0
                )
            term = term * taps_ref[pl.ds(offset, 1), :].astype(jnp.float32)
            summed = term if summed is None else summed + term
        return summed / (1.0 + jnp.exp(-summed))

    queries_all = short_conv(q_ref, prev_q, cq_ref)
    keys_all = short_conv(k_ref, prev_k, ck_ref)
    values_all = short_conv(v_ref, prev_v, cv_ref)

    for step in range(1, groups):
        source = lax.rem(tp_me + step, groups)
        pltpu.make_async_remote_copy(
            src_ref=partial, dst_ref=got_gate.at[source], send_sem=gate_send.at[0],
            recv_sem=gate_recv.at[source], device_id=(me, source), device_id_type=MESH,
        ).wait_recv()
    gate_total = None
    for source in range(groups):
        term = jnp.where(source == tp_me, partial[...], got_gate[source])
        gate_total = term if gate_total is None else gate_total + term
    lanes = lax.broadcasted_iota(jnp.int32, gate_total.shape, 1)

    seg_grid = jnp.broadcast_to(own_seg, (length, length))
    same = seg_grid == jnp.transpose(seg_grid)
    causal = (rows >= cols) & same
    strict = (rows > cols) & same
    linked = (own_seg == prev_cols[length - 1 :, 0:1]).astype(jnp.float32)
    tail = (own_seg == own_seg[length - 1 :, :]).astype(jnp.float32)
    linked_last = linked[length - 1 :, :]

    def head_terms(h):
        column = tp_me * heads + h
        decay_in = jnp.sum(jnp.where(lanes == column, gate_total, 0.0), axis=1, keepdims=True)
        beta_in = jnp.sum(
            jnp.where(lanes == HEADS + column, gate_total, 0.0), axis=1, keepdims=True
        )
        shifted_in = decay_in + bias_ref[h]
        softplus = jnp.maximum(shifted_in, 0.0) + jnp.log1p(jnp.exp(-jnp.abs(shifted_in)))
        log_alpha = -decay_ref[h] * softplus
        beta = 1.0 / (1.0 + jnp.exp(-beta_in))

        key_raw = keys_all[:, h * DK : (h + 1) * DK]
        values = values_all[:, h * DV : (h + 1) * DV]
        keys = key_raw * lax.rsqrt(jnp.sum(key_raw * key_raw, axis=1, keepdims=True) + 1e-06)
        cum_grid = fold(lower_ones, jnp.broadcast_to(log_alpha, (length, length)))
        cumulative = cum_grid[:, 0:1]
        last = cum_grid[length - 1 :, 0:1]
        gap = cum_grid - jnp.transpose(cum_grid)
        decays = jnp.where(causal, jnp.exp(jnp.where(causal, gap, 0.0)), 0.0)
        coupling = beta * fold_t(keys, keys) * jnp.where(strict, decays, 0.0)
        inverse = inverse_unit_lower(coupling, eye)
        start_scale = jnp.exp(cumulative) * linked
        fresh = fold(inverse, beta * values)
        carried = fold(inverse, (beta * start_scale) * keys)
        fade_out = jnp.exp(last - cumulative) * tail
        pushed_t = jnp.transpose(fade_out * keys)
        keep = linked_last * jnp.exp(last)
        carry_sc[h] = keep * eye - fold(pushed_t, carried)
        inject_sc[h] = fold(pushed_t, fresh)
        keys_sc[h] = keys
        decay_sc[h] = decays
        start_sc[h] = jnp.broadcast_to(start_scale, (length, DK))
        fresh_sc[h] = fresh
        carried_sc[h] = carried

    def head_outputs(h):
        queries = queries_all[:, h * DK : (h + 1) * DK]
        scores = fold_t(queries, keys_sc[h]) * decay_sc[h]
        reach_sc[h] = queries * start_sc[h] - fold(scores, carried_sc[h])
        local_sc[h] = fold(scores, fresh_sc[h])

    def remote(step, slot, src, dst, target):
        return pltpu.make_async_remote_copy(
            src_ref=src, dst_ref=dst,
            send_sem=send_sems.at[step, slot], recv_sem=recv_sems.at[step, slot],
            device_id=at(target), device_id_type=MESH,
        )

    def launch(step, pairs, shift):
        copies = [remote(step, slot, src, dst, me + shift) for slot, (src, dst) in enumerate(pairs)]

        @pl.when(me + shift < devices)
        def _():
            for copy in copies:
                copy.start()

        return copies

    def land(copies, pairs, shift):
        @pl.when(me >= shift)
        def _():
            for copy in copies:
                copy.wait_recv()

        @pl.when(me < shift)
        def _():
            for _, dst in pairs:
                dst[...] = jnp.zeros(dst.shape, dst.dtype)

        return copies

    def sent(copies, shift):
        @pl.when(me + shift < devices)
        def _():
            for copy in copies:
                copy.wait_send()

    first = [
        remote(0, 0, carry_sc.at[1 - core], got1_a, partner),
        remote(0, 1, inject_sc.at[1 - core], got1_b, partner),
    ]
    for own_head in range(heads):

        @pl.when(core == own_head)
        def _():
            head_terms(1 - own_head)
            for copy in first:
                copy.start()
            head_terms(own_head)

    for copy in gate_copies:
        copy.wait_send()

    @pl.when(me + 1 < devices)
    def _():
        for copy in edge_copies:
            copy.wait_send()

    for copy in first:
        copy.wait_recv()
    own_a = carry_sc[core]
    own_b = inject_sc[core]
    low = core == 0
    lo_a[...] = jnp.where(low, own_a, got1_a[...])
    lo_b[...] = jnp.where(low, own_b, got1_b[...])
    hi_a = jnp.where(low, got1_a[...], own_a)
    hi_b = jnp.where(low, got1_b[...], own_b)
    join_a[...] = fold(hi_a, lo_a[...])
    join_b[...] = fold(hi_a, lo_b[...]) + hi_b
    wire_a[...] = join_a[...].astype(wire_a.dtype)
    wire_b[...] = join_b[...].astype(wire_b.dtype)
    for copy in first:
        copy.wait_send()

    pairs = ((wire_a, got2_a), (wire_b, got2_b))
    copies = launch(1, pairs, 2)
    head_outputs(0)
    land(copies, pairs, 2)
    pair_a[...] = fold(join_a[...], got2_a[...].astype(jnp.float32))
    pair_b[...] = fold(join_a[...], got2_b[...].astype(jnp.float32)) + join_b[...]
    wire_pair[...] = pair_b[...].astype(wire_pair.dtype)
    sent(copies, 2)

    pairs = ((wire_pair, got3_b),)
    copies = launch(2, pairs, 4)
    head_outputs(1)
    land(copies, pairs, 4)
    quad_b[...] = fold(pair_a[...], got3_b[...].astype(jnp.float32)) + pair_b[...]
    wire_quad[...] = quad_b[...].astype(wire_quad.dtype)
    sent(copies, 4)

    pairs = ((wire_quad, got4_b),)
    copies = launch(3, pairs, 2)
    land(copies, pairs, 2)
    entering = got4_b[...].astype(jnp.float32)
    onward = fold(lo_a[...], entering) + lo_b[...]
    sent(copies, 2)

    reply[...] = jnp.where(low, onward, entering)
    last_copy = remote(4, 0, reply, incoming.at[core], partner)
    last_copy.start()
    incoming[core] = jnp.where(low, entering, onward)
    remote(4, 0, reply, incoming.at[1 - core], partner).wait_recv()

    gain = gain_ref[...].astype(jnp.float32)
    for h in range(heads):
        head_out = local_sc[h] + fold(reach_sc[h], incoming[h])
        scale = lax.rsqrt(jnp.mean(head_out * head_out, axis=1, keepdims=True) + 1e-06)
        z_part = z_ref[:, h * DV : (h + 1) * DV].astype(jnp.float32)
        gating = z_part / (1.0 + jnp.exp(-z_part))
        out_ref[:, h * DV : (h + 1) * DV] = (head_out * scale * gain * gating).astype(
            out_ref.dtype
        )
    last_copy.wait_send()


def local(
    layer_input, q_in, k_in, v_in, z_in, conv_q, conv_k, conv_v,
    gate_weight, decay_rate, dt_bias, norm_gain, segment_ids,
):
    length = q_in.shape[0]
    heads = q_in.shape[1] // DK
    devices = lax.axis_size("req")
    groups = lax.axis_size("tp")
    f32 = jnp.float32
    a_shape = pltpu.VMEM((DK, DK), f32)
    b_shape = pltpu.VMEM((DK, DV), f32)
    a_wire = pltpu.VMEM((DK, DK), jnp.bfloat16)
    b_wire = pltpu.VMEM((DK, DV), jnp.bfloat16)
    vmem = pl.BlockSpec(memory_space=pltpu.VMEM)
    smem = pl.BlockSpec(memory_space=pltpu.SMEM)
    return pl.pallas_call(
        functools.partial(layer_kernel, devices, groups),
        out_shape=jax.ShapeDtypeStruct(z_in.shape, jnp.bfloat16),
        in_specs=[vmem] * 9 + [smem, smem, vmem, vmem],
        out_specs=vmem,
        scratch_shapes=[
            pltpu.VMEM((length, gate_weight.shape[1]), f32),
            pltpu.VMEM((groups, length, gate_weight.shape[1]), f32),
            pltpu.VMEM(q_in.shape, q_in.dtype),
            pltpu.VMEM(k_in.shape, k_in.dtype),
            pltpu.VMEM(v_in.shape, v_in.dtype),
            pltpu.VMEM((1, length), segment_ids.dtype),
            pltpu.VMEM((heads, length, DV), f32),
            pltpu.VMEM((heads, length, DK), f32),
            pltpu.VMEM((heads, DK, DK), f32),
            pltpu.VMEM((heads, DK, DV), f32),
            pltpu.VMEM((heads, DK, DV), f32),
            pltpu.VMEM((heads, length, DK), f32),
            pltpu.VMEM((heads, length, length), f32),
            pltpu.VMEM((heads, length, DK), f32),
            pltpu.VMEM((heads, length, DV), f32),
            pltpu.VMEM((heads, length, DK), f32),
            a_shape, b_shape, a_wire, b_wire, b_wire, b_wire,
            a_shape, b_shape, a_shape, b_shape, a_shape, b_shape, b_shape, b_shape,
            a_wire, b_wire, b_wire, b_wire,
            pltpu.SemaphoreType.DMA((groups,)),
            pltpu.SemaphoreType.DMA((groups,)),
            pltpu.SemaphoreType.DMA((4,)),
            pltpu.SemaphoreType.DMA((4,)),
            pltpu.SemaphoreType.DMA((5, 2)),
            pltpu.SemaphoreType.DMA((5, 2)),
        ],
        compiler_params=pltpu.CompilerParams(collective_id=0, has_side_effects=True),
    )(
        layer_input, gate_weight, q_in, k_in, v_in, z_in, conv_q, conv_k, conv_v,
        decay_rate, dt_bias, norm_gain.reshape(1, -1), segment_ids.reshape(1, -1),
    )


def solution(mesh):
    placed = (
        P("req", "tp"),
        P("req", "tp"),
        P("req", "tp"),
        P("req", "tp"),
        P("req", "tp"),
        P(None, "tp"),
        P(None, "tp"),
        P(None, "tp"),
        P("tp", None),
        P("tp"),
        P("tp"),
        P(),
        P("req"),
    )
    return jax.shard_map(
        local, mesh=mesh, in_specs=placed, out_specs=P("req", "tp"), check_vma=False
    )
```
